32 devices in a mesh: groups: 2 (over y), seq: 4 (over z), grid: 4 (over x, core).
Axes of the slice: x: 2, y: 2, z: 4, core: 2. Of those that a mesh axis runs over, the one named last changes fastest.
Arguments:
- queries: bfloat16 [16384, 2048], P(('groups', 'seq'), 'grid'), parts along dimension 0, may hold values from -6 to 6
- keys: bfloat16 [16384, 1024], P(('groups', 'seq'), 'grid'), parts along dimension 0, may hold values from -6 to 6
- values: bfloat16 [16384, 1024], P(('groups', 'seq'), 'grid'), parts along dimension 0, may hold values from -6 to 6
- out_grad: bfloat16 [16384, 2048], P(('groups', 'seq'), 'grid'), parts along dimension 0, may hold values from -6 to 6
- layer_input: bfloat16 [16384, 2048], P(('groups', 'seq')), parts along dimension 0, may hold values from -6 to 6
- moment: bfloat16 [64, 512, 512], P(('groups', 'grid'), 'seq'), parts along dimension 0, may hold values from -6 to 6
- left_old: bfloat16 [64, 512, 512], P(('groups', 'grid'), 'seq'), parts along dimension 0, may hold values from -0.25 to 0.25
- left_new: bfloat16 [64, 512, 512], P(('groups', 'grid'), 'seq'), parts along dimension 0, may hold values from -0.25 to 0.25
- right_old: bfloat16 [64, 512, 512], P(('groups', 'grid'), 'seq'), parts along dimension 0, may hold values from -0.25 to 0.25
- right_new: bfloat16 [64, 512, 512], P(('groups', 'grid'), 'seq'), parts along dimension 0, may hold values from -0.25 to 0.25
Outputs:
- attention_out: bfloat16 [16384, 2048], P(('groups', 'seq'), 'grid'), parts along dimension 0
- query_grad: bfloat16 [16384, 2048], P(('groups', 'seq'), 'grid'), parts along dimension 0
- key_grad: bfloat16 [16384, 1024], P(('groups', 'seq'), 'grid'), parts along dimension 0
- value_grad: bfloat16 [16384, 1024], P(('groups', 'seq'), 'grid'), parts along dimension 0
- new_moment: float32 [64, 512, 512], P(('groups', 'grid'), 'seq'), parts along dimension 0
The draws below stay inside these ranges and needn't reach their ends.
There are 2 independent parts, one for each index of `groups`. The reference program is written for one: setup_inputs(seed, part) draws one part's arguments, and reference() takes and returns one part's arrays. A program takes and returns all parts, laid end to end along the dimension named above; each array names one. Nothing has to cross between parts.
All inputs are finite; a program needn't handle non-finite values.
Results may differ from the reference program's by a relative error of at most 0.024.
Values may be sent and summed in bfloat16 or wider, within the bound.
No kernel may reach another device: no remote copies, remote signals or barrier semaphores. Data moves between devices by JAX's collectives and lax.ppermute only.
A program may use at most 640 MiB of HBM per device.

```python
import jax
import jax.numpy as jnp
from jax import lax

HEAD_DIM = 128
KV_HEADS = 8
GROUP = 2
Q_HEADS = 16
WINDOW = 4096
T_DEV = 2048
TOKENS = 8192
ROWS_IN = 2048
JOINED = 4096
BLOCK = 512
NBLK = 32


def draw_queries(key, part):
    base_draw = jnp.clip(jax.random.normal(jax.random.fold_in(key, 1), (TOKENS, Q_HEADS * HEAD_DIM), jnp.float32), -5.0, 5.0)
    return base_draw.astype(jnp.bfloat16)


def draw_keys(key, part):
    base_draw = jnp.clip(jax.random.normal(jax.random.fold_in(key, 2), (TOKENS, KV_HEADS * HEAD_DIM), jnp.float32), -5.0, 5.0)
    return base_draw.astype(jnp.bfloat16)


def level_of(stream_key, dims, pieces, smallest, high):
    def one(dim, blocks):
        draws = jax.random.uniform(jax.random.fold_in(jax.random.fold_in(stream_key, 6), dim), (blocks,), jnp.float32, smallest / len(pieces), high / len(pieces))
        return jnp.repeat(jnp.exp(draws), dims[dim] // blocks).reshape((-1,) + (1,) * (len(dims) - dim - 1))

    gain = one(*pieces[0])
    for cut in pieces[1:]:
        gain = gain * one(*cut)
    return gain


def gaussian(rng, shape, scale, reach, shards=(), held_as=jnp.bfloat16):
    values = scale * jax.random.normal(rng, shape, jnp.float32)
    if shards:
        values = values * level_of(rng, shape, shards, -0.22, 0.18)
    return jnp.clip(values, -reach, reach).astype(held_as)


def setup_inputs(seed: int = 0, part: int = 0) -> dict:
    arg_keys = jax.random.split(jax.random.key(seed), 11)
    own_keys = jax.random.split(jax.random.fold_in(arg_keys[10], part), 11)
    return {
        "queries": draw_queries(jax.random.fold_in(jax.random.fold_in(arg_keys[10], part), 71), part),
        "keys": draw_keys(jax.random.fold_in(jax.random.fold_in(arg_keys[10], part), 71), part),
        "values": gaussian(own_keys[2], (TOKENS, KV_HEADS * HEAD_DIM), 1.0, 6.0, ((0, 4), (1, 4))),
        "out_grad": gaussian(own_keys[3], (TOKENS, Q_HEADS * HEAD_DIM), 1.0, 6.0, ((0, 4), (1, 4))),
        "layer_input": gaussian(own_keys[4], (TOKENS, ROWS_IN), 1.0, 6.0, ((0, 4),)),
        "moment": gaussian(own_keys[5], (NBLK, BLOCK, BLOCK), 1.0, 6.0, ((0, 4), (1, 4))),
        "left_old": gaussian(own_keys[6], (NBLK, BLOCK, BLOCK), BLOCK ** -0.5, 0.25, ((0, 4), (1, 4))),
        "left_new": gaussian(own_keys[7], (NBLK, BLOCK, BLOCK), BLOCK ** -0.5, 0.25, ((0, 4), (1, 4))),
        "right_old": gaussian(own_keys[8], (NBLK, BLOCK, BLOCK), BLOCK ** -0.5, 0.25, ((0, 4), (1, 4))),
        "right_new": gaussian(own_keys[9], (NBLK, BLOCK, BLOCK), BLOCK ** -0.5, 0.25, ((0, 4), (1, 4))),
    }


moment_decay = 0.8


def head_pass(q_block, k_block, v_block, g_block):
    score_scale = HEAD_DIM ** -0.5
    zero_rows = jnp.zeros((WINDOW, HEAD_DIM), jnp.bfloat16)
    k_padded = jnp.concatenate([zero_rows, k_block], axis=0)
    v_padded = jnp.concatenate([zero_rows, v_block], axis=0)
    window_rows = WINDOW + T_DEV
    key_index = jnp.arange(window_rows, dtype=jnp.int32)
    query_index = jnp.arange(T_DEV, dtype=jnp.int32)

    def one_block(acc_pair, block_index):
        key_acc, value_acc = acc_pair
        block_start = (block_index * T_DEV).astype(jnp.int32)
        q_rows = lax.dynamic_slice_in_dim(q_block, block_start, T_DEV, 0)
        g_rows = lax.dynamic_slice_in_dim(g_block, block_start, T_DEV, 0)
        k_rows = lax.dynamic_slice_in_dim(k_padded, block_start, window_rows, 0)
        v_rows = lax.dynamic_slice_in_dim(v_padded, block_start, window_rows, 0)
        key_pos = block_start - WINDOW + key_index
        query_pos = block_start + query_index
        distance = query_pos[:, None] - key_pos[None, :]
        visible = (distance >= 0) & (distance < WINDOW) & (key_pos[None, :] >= 0)
        scores = jnp.where(visible, jnp.dot(q_rows, k_rows.T, preferred_element_type=jnp.float32) * score_scale, -jnp.inf)
        row_max = jnp.max(scores, axis=1, keepdims=True)
        log_total = row_max + jnp.log(jnp.sum(jnp.exp(scores - row_max), axis=1, keepdims=True))
        weights = jnp.exp(scores - log_total)
        weights_bf = weights.astype(jnp.bfloat16)
        head_out = jnp.dot(weights_bf, v_rows, preferred_element_type=jnp.float32).astype(jnp.bfloat16)
        row_dot = jnp.sum(g_rows.astype(jnp.float32) * head_out.astype(jnp.float32), axis=1, keepdims=True)
        weight_grad = jnp.dot(g_rows, v_rows.T, preferred_element_type=jnp.float32)
        score_grad = (weights * (weight_grad - row_dot) * score_scale).astype(jnp.bfloat16)
        query_grad = jnp.dot(score_grad, k_rows, preferred_element_type=jnp.float32).astype(jnp.bfloat16)
        key_part = jnp.dot(score_grad.T, q_rows, preferred_element_type=jnp.float32)
        value_part = jnp.dot(weights_bf.T, g_rows, preferred_element_type=jnp.float32)
        old_keys = lax.dynamic_slice_in_dim(key_acc, block_start, window_rows, 0)
        key_acc = lax.dynamic_update_slice_in_dim(key_acc, old_keys + key_part, block_start, 0)
        old_values = lax.dynamic_slice_in_dim(value_acc, block_start, window_rows, 0)
        value_acc = lax.dynamic_update_slice_in_dim(value_acc, old_values + value_part, block_start, 0)
        return (key_acc, value_acc), (head_out, query_grad)

    start_pair = (jnp.zeros((TOKENS + WINDOW, HEAD_DIM), jnp.float32), jnp.zeros((TOKENS + WINDOW, HEAD_DIM), jnp.float32))
    final_pair, block_outs = lax.scan(one_block, start_pair, jnp.arange(TOKENS // T_DEV, dtype=jnp.int32))
    head_out = block_outs[0].reshape(TOKENS, HEAD_DIM)
    query_grad = block_outs[1].reshape(TOKENS, HEAD_DIM)
    return head_out, query_grad, final_pair[0][WINDOW:], final_pair[1][WINDOW:]


def rotate_block(block_args):
    moment_block, left_before, left_after, right_before, right_after, grad_block = block_args
    right_turn = jnp.dot(right_before.T, right_after, preferred_element_type=jnp.float32).astype(jnp.bfloat16)
    turned = jnp.dot(moment_block, right_turn, preferred_element_type=jnp.float32).astype(jnp.bfloat16)
    carried = jnp.dot(left_before, turned, preferred_element_type=jnp.float32)
    grad_turned = jnp.dot(grad_block, right_after, preferred_element_type=jnp.float32)
    inner = (moment_decay * carried + (1.0 - moment_decay) * grad_turned).astype(jnp.bfloat16)
    return jnp.dot(left_after.T, inner, preferred_element_type=jnp.float32)


def reference(queries, keys, values, out_grad, layer_input, moment, left_old, left_new, right_old, right_new):
    def head_at(q_head):
        kv_slot = q_head // GROUP
        q_block = lax.dynamic_slice_in_dim(queries, q_head * HEAD_DIM, HEAD_DIM, 1)
        g_block = lax.dynamic_slice_in_dim(out_grad, q_head * HEAD_DIM, HEAD_DIM, 1)
        k_block = lax.dynamic_slice_in_dim(keys, kv_slot * HEAD_DIM, HEAD_DIM, 1)
        v_block = lax.dynamic_slice_in_dim(values, kv_slot * HEAD_DIM, HEAD_DIM, 1)
        return head_pass(q_block, k_block, v_block, g_block)

    head_outs, query_grads, key_parts, value_parts = lax.map(head_at, jnp.arange(Q_HEADS, dtype=jnp.int32))
    attention_out = jnp.transpose(head_outs, (1, 0, 2)).reshape(TOKENS, Q_HEADS * HEAD_DIM)
    query_grad = jnp.transpose(query_grads, (1, 0, 2)).reshape(TOKENS, Q_HEADS * HEAD_DIM)
    key_sums = jnp.sum(key_parts.reshape(KV_HEADS, GROUP, TOKENS, HEAD_DIM), axis=1)
    value_sums = jnp.sum(value_parts.reshape(KV_HEADS, GROUP, TOKENS, HEAD_DIM), axis=1)
    key_grad = jnp.transpose(key_sums, (1, 0, 2)).reshape(TOKENS, KV_HEADS * HEAD_DIM).astype(jnp.bfloat16)
    value_grad = jnp.transpose(value_sums, (1, 0, 2)).reshape(TOKENS, KV_HEADS * HEAD_DIM).astype(jnp.bfloat16)
    joined_grad = jnp.concatenate([query_grad.reshape(TOKENS, KV_HEADS, GROUP * HEAD_DIM), key_grad.reshape(TOKENS, KV_HEADS, HEAD_DIM), value_grad.reshape(TOKENS, KV_HEADS, HEAD_DIM)], axis=2).reshape(TOKENS, JOINED)
    projection_grad = jnp.dot(layer_input.T, joined_grad, preferred_element_type=jnp.float32).astype(jnp.bfloat16)
    row_blocks = ROWS_IN // BLOCK
    col_blocks = JOINED // BLOCK
    grad_block = jnp.transpose(projection_grad.reshape(row_blocks, BLOCK, col_blocks, BLOCK), (2, 0, 1, 3)).reshape(NBLK, BLOCK, BLOCK)
    new_moment = lax.map(rotate_block, (moment, left_old, left_new, right_old, right_new, grad_block))
    return attention_out, query_grad, key_grad, value_grad, new_moment
```

```python
import functools

import jax
import jax.numpy as jnp
from jax import lax
from jax.experimental import pallas as pl
from jax.experimental.pallas import tpu as pltpu
from jax.sharding import PartitionSpec as P

HEAD_DIM = 128
NEG = -1e30
LOG2E = 1.4426950408889634
NT = (((1,), (1,)), ((), ()))
NN = (((1,), (0,)), ((), ()))


def mm(a, b, dims):
    return lax.dot_general(a, b, dims, preferred_element_type=jnp.float32)


def attn_body(reach, tile, group, bk, q_ref, g_ref, bias_ref, *rest):
    kv_refs = rest[: reach + 1]
    o_ref, dq_ref, far_ref, own_ref, kb, vb, kt, vt, s_buf, e_buf, dkt, dvt = rest[reach + 1:]
    hd = HEAD_DIM
    t = pl.program_id(0)
    rows = kv_refs[0].shape[0]
    win = reach * rows
    cols = group * tile
    scale = hd ** -0.5

    @pl.when(t == 0)
    def _():
        for s, ref in enumerate(kv_refs):
            here = pl.ds(s * rows, rows)
            k = ref[:, :hd]
            v = ref[:, hd:]
            kb[here, :hd] = k
            kb[here, hd:] = bias_ref[here, :]
            vb[here, :] = v
            kt[:, here] = k.T
            vt[:hd, here] = v.T
        vt[hd:, :] = jnp.ones((16, win + rows), jnp.bfloat16)
        dkt[...] = jnp.zeros_like(dkt)
        dvt[...] = jnp.zeros_like(dvt)

    q = jnp.concatenate([q_ref[:, h * hd:(h + 1) * hd] for h in range(group)], axis=0)
    g = jnp.concatenate([g_ref[:, h * hd:(h + 1) * hd] for h in range(group)], axis=0)
    lane = lax.broadcasted_iota(jnp.int32, (cols, hd), 1)
    qa = jnp.concatenate([q, jnp.where(lane == 0, 1.0, 0.0).astype(jnp.bfloat16)], axis=1)
    base = t * tile
    n_full = win - tile

    ki = lax.broadcasted_iota(jnp.int32, (tile, cols), 0)
    qi = lax.broadcasted_iota(jnp.int32, (tile, cols), 1) % tile

    def scores(off, size, keep=None):
        at = pl.ds(pl.multiple_of(base + off, tile), size)
        s = mm(kb[at, :], qa, NT)
        if keep is not None:
            s = jnp.where(keep, s, NEG)
        s_buf[pl.ds(off, size), :] = s
        return jnp.max(s.reshape(size // 8, 8, cols), axis=0)

    m8 = jnp.maximum(scores(0, tile, ki > qi), scores(win, tile, ki <= qi))
    m8 = lax.fori_loop(
        0, n_full // bk,
        lambda i, m: jnp.maximum(m, scores(pl.multiple_of(tile + i * bk, tile), bk)), m8)
    m = jnp.max(m8, axis=0, keepdims=True)
    mc = m * (scale * LOG2E)

    def weigh(off, size):
        at = pl.ds(pl.multiple_of(base + off, tile), size)
        e = jnp.exp2(s_buf[pl.ds(off, size), :] * (scale * LOG2E) - mc).astype(jnp.bfloat16)
        e_buf[pl.ds(off, size), :] = e
        return mm(vt[:, at], e, NN)

    ot = weigh(0, tile) + weigh(win, tile)
    ot = lax.fori_loop(
        0, n_full // bk,
        lambda i, a: a + weigh(pl.multiple_of(tile + i * bk, tile), bk), ot)
    rl = 1.0 / ot[hd:hd + 1, :]
    on = (ot[:hd, :] * rl).astype(jnp.bfloat16)
    on32 = on.astype(jnp.float32)
    gt = g.astype(jnp.float32).T
    qt = q.astype(jnp.float32).T
    dd = jnp.sum(gt * on32, axis=0, keepdims=True)
    for h in range(group):
        o_ref[:, h * hd:(h + 1) * hd] = on32[:, h * tile:(h + 1) * tile].T.astype(jnp.bfloat16)
    glt = (gt * rl).astype(jnp.bfloat16)
    rs = rl * scale
    qrt = (qt * rs).astype(jnp.bfloat16)

    def back(off, size):
        at = pl.ds(pl.multiple_of(base + off, tile), size)
        e = e_buf[pl.ds(off, size), :]
        dp = mm(vb[at, :], g, NT) - dd
        ds = (e.astype(jnp.float32) * dp).astype(jnp.bfloat16)
        dvt[:, at] += mm(glt, e, NT)
        dkt[:, at] += mm(qrt, ds, NT)
        return mm(kt[:, at], ds, NN)

    dqt = back(0, tile) + back(win, tile)
    dqt = lax.fori_loop(
        0, n_full // bk,
        lambda i, a: a + back(pl.multiple_of(tile + i * bk, tile), bk), dqt)
    dqt = dqt * rs
    for h in range(group):
        dq_ref[:, h * hd:(h + 1) * hd] = dqt[:, h * tile:(h + 1) * tile].T.astype(jnp.bfloat16)

    @pl.when(t == pl.num_programs(0) - 1)
    def _():
        for s in range(reach + 1):
            here = pl.ds(s * rows, rows)
            dk = dkt[:, here].T
            dv = dvt[:, here].T
            if s < reach:
                far_ref[here, :hd] = dk.astype(jnp.bfloat16)
                far_ref[here, hd:] = dv.astype(jnp.bfloat16)
            else:
                own_ref[:, :hd] = dk
                own_ref[:, hd:] = dv


def attention(queries, out_grad, bias, shards, slot, group, tile=256, bk=1920):
    hd = HEAD_DIM
    rows = queries.shape[0]
    reach = len(shards) - 1
    win = reach * rows
    total = win + rows
    cols = group * tile
    while (win - tile) % bk:
        bk -= tile
    whole = lambda shape: pl.BlockSpec(shape, lambda t: (0, 0), pipeline_mode=pl.Buffered(1))
    part = pl.BlockSpec((tile, group * hd), lambda t: (t, slot))
    outp = pl.BlockSpec((tile, group * hd), lambda t: (t, 0))
    area = win * rows * group
    return pl.pallas_call(
        functools.partial(attn_body, reach, tile, group, bk),
        out_shape=(
            jax.ShapeDtypeStruct((rows, group * hd), jnp.bfloat16),
            jax.ShapeDtypeStruct((rows, group * hd), jnp.bfloat16),
            jax.ShapeDtypeStruct((win, 2 * hd), jnp.bfloat16),
            jax.ShapeDtypeStruct((rows, 2 * hd), jnp.float32),
        ),
        grid=(rows // tile,),
        in_specs=[part, part, whole((total, hd))] + [whole((rows, 2 * hd))] * (reach + 1),
        out_specs=(outp, outp, whole((win, 2 * hd)), whole((rows, 2 * hd))),
        scratch_shapes=[
            pltpu.VMEM((total, 2 * hd), jnp.bfloat16),
            pltpu.VMEM((total, hd), jnp.bfloat16),
            pltpu.VMEM((hd, total), jnp.bfloat16),
            pltpu.VMEM((hd + 16, total), jnp.bfloat16),
            pltpu.VMEM((win + tile, cols), jnp.float32),
            pltpu.VMEM((win + tile, cols), jnp.bfloat16),
            pltpu.VMEM((hd, total), jnp.float32),
            pltpu.VMEM((hd, total), jnp.float32),
        ],
        compiler_params=pltpu.CompilerParams(
            dimension_semantics=("arbitrary",), vmem_limit_bytes=60 << 20),
        cost_estimate=pl.CostEstimate(
            flops=12 * area * hd, bytes_accessed=16 << 20, transcendentals=area),
        name="window_attention",
    )(queries, out_grad, bias, *shards)


moment_decay = 0.8


def shifted(x, axis, by):
    length = lax.axis_size(axis)
    pairs = [(i, i + by) for i in range(length) if 0 <= i + by < length]
    return lax.ppermute(x, axis, pairs)


def after(value, *others):
    return lax.optimization_barrier((value,) + others)[0]


def row_split_refresh(grad_term_sum, moment, left_old, left_new, right_old, right_new):
    turn_share = lax.psum_scatter(
        jnp.einsum("brk,brj->kbj", right_old, right_new, preferred_element_type=jnp.float32),
        "seq", scatter_dimension=0, tiled=True)
    right_turn = jnp.transpose(turn_share, (1, 0, 2)).astype(jnp.bfloat16)
    turned = jnp.einsum(
        "brk,bkj->brj", moment, lax.all_gather(right_turn, "seq", axis=1, tiled=True),
        preferred_element_type=jnp.float32).astype(jnp.bfloat16)
    carried = jnp.einsum(
        "brk,bkj->brj", left_old, lax.all_gather(turned, "seq", axis=1, tiled=True),
        preferred_element_type=jnp.float32)
    grad_term = jnp.einsum(
        "brk,bkj->brj", grad_term_sum, lax.all_gather(right_new, "seq", axis=1, tiled=True),
        preferred_element_type=jnp.float32)
    inner = (moment_decay * carried + (1.0 - moment_decay) * grad_term).astype(jnp.bfloat16)
    new_share = lax.psum_scatter(
        jnp.einsum("brk,brj->kbj", left_new, inner, preferred_element_type=jnp.float32),
        "seq", scatter_dimension=0, tiled=True)
    return jnp.transpose(new_share, (1, 0, 2))


def bmm(spec, a, b):
    return jnp.einsum(spec, a, b, preferred_element_type=jnp.float32)


def per_device(
    queries, keys, values, out_grad, layer_input, moment, left_old, left_new, right_old, right_new
):
    n = lax.axis_size("seq")
    reach = n // 2
    seq_index = lax.axis_index("seq")
    rows = queries.shape[0]
    hd = HEAD_DIM
    kv_count = keys.shape[1] // hd
    group = queries.shape[1] // keys.shape[1]
    blocks, share_rows, order = moment.shape
    row_blocks = layer_input.shape[1] // order
    whole_blocks = row_blocks % n == 0 and (group + 2) * hd == order
    per_owner = row_blocks // n

    pairs = [
        jnp.concatenate([keys[:, k * hd:(k + 1) * hd], values[:, k * hd:(k + 1) * hd]], axis=1)
        for k in range(kv_count)
    ]
    key_row = lax.broadcasted_iota(jnp.int32, ((reach + 1) * rows, hd), 0)
    key_col = lax.broadcasted_iota(jnp.int32, ((reach + 1) * rows, hd), 1)
    bias = jnp.where(
        (key_row < (reach - seq_index) * rows) & (key_col == 0), NEG, 0.0).astype(jnp.bfloat16)

    windows = []
    gate = None
    for k in range(kv_count):
        held = pairs[k] if gate is None else after(pairs[k], gate)
        shards = [pairs[k]]
        if k == 0:
            for _ in range(reach):
                held = shifted(held, "seq", 1)
                shards.insert(0, held)
            gate = held
        else:
            for d in range(1, reach + 1):
                shards.insert(0, shifted(held, "seq", d))
        windows.append(shards)

    if whole_blocks:
        cut = [
            x.reshape(kv_count, n, per_owner, share_rows, order)
            for x in (moment, left_old, left_new, right_old, right_new)
        ]

        def message(owner):
            return jnp.stack([
                lax.dynamic_slice_in_dim(x, owner, 1, 1)[:, 0] for x in cut])

        whole = jnp.zeros((5, kv_count, per_owner, n, share_rows, order), jnp.bfloat16)
        whole = lax.dynamic_update_slice_in_dim(
            whole, message(seq_index)[:, :, :, None], seq_index, 3)
        leftward = []
        for d in range(1, n):
            packed = after(message((seq_index + n - d) % n), windows[0][reach - 1])
            leftward.append(shifted(packed, "seq", -d))
        rightward = []
    outs, query_grads, key_grads, value_grads, news, joined = [], [], [], [], [], []
    for k in range(kv_count):
        mask = after(bias, *leftward) if whole_blocks and k == 1 else bias
        head_out, head_dq, far, own = attention(
            queries, out_grad, mask, windows[k], k, group)
        if whole_blocks and k == 0:
            for d in range(1, n):
                packed = after(message((seq_index + d) % n), head_out)
                rightward.append(shifted(packed, "seq", d))
        outs.append(head_out)
        query_grads.append(head_dq)
        own = own.astype(jnp.float32)
        if k < kv_count - 1:
            for d in range(1, reach + 1):
                back = shifted(far[(reach - d) * rows:(reach - d + 1) * rows], "seq", -d)
                own = own + back.astype(jnp.float32)
        else:
            carry = far[:rows]
            for d in range(reach, 0, -1):
                carry = shifted(carry, "seq", -1)
                if whole_blocks and d == reach:
                    carry = after(carry, *rightward)
                carry = carry.astype(jnp.float32)
                if d > 1:
                    carry = (carry + far[(reach - d + 1) * rows:(reach - d + 2) * rows].astype(jnp.float32)).astype(jnp.bfloat16)
            own = own + carry
        kv_grad = own.astype(jnp.bfloat16)
        key_grads.append(kv_grad[:, :hd])
        value_grads.append(kv_grad[:, hd:])
        columns = jnp.concatenate([head_dq, kv_grad], axis=1)
        joined.append(columns)
        if whole_blocks and k == 0:
            for d in range(1, n):
                source = (seq_index + d) % n
                piece = jnp.where(seq_index + d < n, leftward[d - 1], rightward[n - d - 1])
                whole = lax.dynamic_update_slice_in_dim(whole, piece[:, :, :, None], source, 3)
            m_own, lo_own, ln_own, ro_own, rn_own = whole.reshape(
                5, kv_count, per_owner, order, order)
            right_turn = bmm("cbrk,cbrj->cbkj", ro_own, rn_own).astype(jnp.bfloat16)
            turned = bmm("cbrk,cbkj->cbrj", m_own, right_turn).astype(jnp.bfloat16)
            carried = moment_decay * bmm("cbrk,cbkj->cbrj", lo_own, turned)
        if whole_blocks:
            term = bmm("tk,tj->kj", layer_input, columns).astype(jnp.bfloat16)
            terms = lax.all_to_all(term.reshape(n, per_owner, order, order), "seq", 0, 0)
            grad = jnp.sum(terms.astype(jnp.float32), axis=0).astype(jnp.bfloat16)
            inner = carried[k] + (1.0 - moment_decay) * bmm("brk,bkj->brj", grad, rn_own[k])
            new = bmm("brk,brj->bkj", ln_own[k], inner.astype(jnp.bfloat16)).astype(jnp.bfloat16)
            new = jnp.transpose(new.reshape(per_owner, n, share_rows, order), (1, 0, 2, 3))
            new = lax.all_to_all(new, "seq", 0, 0)
            news.append(new.reshape(row_blocks, share_rows, order).astype(jnp.float32))
    if whole_blocks:
        new_moment = jnp.concatenate(news, axis=0)
    else:
        joined = jnp.concatenate(joined, axis=1)
        term = bmm(
            "trk,tcj->kcrj",
            layer_input.reshape(rows, row_blocks, order),
            joined.reshape(rows, joined.shape[1] // order, order))
        share = lax.psum_scatter(
            term.reshape(order, blocks, order), "seq", scatter_dimension=0, tiled=True)
        new_moment = row_split_refresh(
            jnp.transpose(share, (1, 0, 2)).astype(jnp.bfloat16),
            moment, left_old, left_new, right_old, right_new)
    join = lambda parts: parts[0] if len(parts) == 1 else jnp.concatenate(parts, axis=1)
    return (join(outs), join(query_grads), join(key_grads), join(value_grads), new_moment)


def solution(mesh):
    both = P(("groups", "seq"), "grid")
    block = P(("groups", "grid"), "seq", None)
    return jax.shard_map(
        per_device,
        mesh=mesh,
        in_specs=(both, both, both, both, P(("groups", "seq"), None)) + (block,) * 5,
        out_specs=(both, both, both, both, block),
        check_vma=False,
    )
```

```python
import functools

import jax
import jax.numpy as jnp
from jax import lax
from jax.experimental import pallas as pl
from jax.experimental.pallas import tpu as pltpu
from jax.sharding import PartitionSpec as P

HEAD_DIM = 128
NEG = -1e30
LOG2E = 1.4426950408889634
NT = (((1,), (1,)), ((), ()))
NN = (((1,), (0,)), ((), ()))


def mm(a, b, dims):
    return lax.dot_general(a, b, dims, preferred_element_type=jnp.float32)


def attn_body(reach, tile, group, bk, skip_ref, q_ref, g_ref, *rest):
    kv_refs = rest[: reach + 1]
    o_ref, dq_ref = rest[reach + 1: reach + 3]
    far_refs = rest[reach + 3: 2 * reach + 3]
    own_ref, kb, vb, kt, vt, s_buf, e_buf, dkt, dvt = rest[2 * reach + 3:]
    hd = HEAD_DIM
    t = pl.program_id(0)
    rows = kv_refs[0].shape[0]
    win = reach * rows
    cols = group * tile
    scale = hd ** -0.5

    @pl.when(t == 0)
    def _():
        first = lax.broadcasted_iota(jnp.int32, (rows, hd), 1) == 0
        for s, ref in enumerate(kv_refs):
            here = pl.ds(s * rows, rows)
            k = ref[:, :hd]
            v = ref[:, hd:]
            kb[here, :hd] = k
            hide = jnp.where(s < skip_ref[0], NEG, 0.0)
            kb[here, hd:] = jnp.where(first, hide, 0.0).astype(jnp.bfloat16)
            vb[here, :] = v
            kt[:, here] = k.T
            vt[:hd, here] = v.T
        vt[hd:, :] = jnp.ones((16, win + rows), jnp.bfloat16)
        dkt[...] = jnp.zeros_like(dkt)
        dvt[...] = jnp.zeros_like(dvt)

    q = jnp.concatenate([q_ref[:, h * hd:(h + 1) * hd] for h in range(group)], axis=0)
    g = jnp.concatenate([g_ref[:, h * hd:(h + 1) * hd] for h in range(group)], axis=0)
    lane = lax.broadcasted_iota(jnp.int32, (cols, hd), 1)
    qa = jnp.concatenate([q, jnp.where(lane == 0, 1.0, 0.0).astype(jnp.bfloat16)], axis=1)
    base = t * tile
    n_full = win - tile

    ki = lax.broadcasted_iota(jnp.int32, (tile, cols), 0)
    qi = lax.broadcasted_iota(jnp.int32, (tile, cols), 1) % tile

    def scores(off, size, keep=None):
        at = pl.ds(pl.multiple_of(base + off, tile), size)
        s = mm(kb[at, :], qa, NT)
        if keep is not None:
            s = jnp.where(keep, s, NEG)
        s_buf[pl.ds(off, size), :] = s
        return jnp.max(s.reshape(size // 8, 8, cols), axis=0)

    m8 = jnp.maximum(scores(0, tile, ki > qi), scores(win, tile, ki <= qi))
    m8 = lax.fori_loop(
        0, n_full // bk,
        lambda i, m: jnp.maximum(m, scores(pl.multiple_of(tile + i * bk, tile), bk)), m8)
    m = jnp.max(m8, axis=0, keepdims=True)
    mc = m * (scale * LOG2E)

    def weigh(off, size):
        at = pl.ds(pl.multiple_of(base + off, tile), size)
        e = jnp.exp2(s_buf[pl.ds(off, size), :] * (scale * LOG2E) - mc).astype(jnp.bfloat16)
        e_buf[pl.ds(off, size), :] = e
        return mm(vt[:, at], e, NN)

    ot = weigh(0, tile) + weigh(win, tile)
    ot = lax.fori_loop(
        0, n_full // bk,
        lambda i, a: a + weigh(pl.multiple_of(tile + i * bk, tile), bk), ot)
    rl = 1.0 / ot[hd:hd + 1, :]
    on = (ot[:hd, :] * rl).astype(jnp.bfloat16)
    on32 = on.astype(jnp.float32)
    gt = g.astype(jnp.float32).T
    qt = q.astype(jnp.float32).T
    dd = jnp.sum(gt * on32, axis=0, keepdims=True)
    for h in range(group):
        o_ref[:, h * hd:(h + 1) * hd] = on32[:, h * tile:(h + 1) * tile].T.astype(jnp.bfloat16)
    glt = (gt * rl).astype(jnp.bfloat16)
    rs = rl * scale
    qrt = (qt * rs).astype(jnp.bfloat16)

    def back(off, size):
        at = pl.ds(pl.multiple_of(base + off, tile), size)
        e = e_buf[pl.ds(off, size), :]
        dp = mm(vb[at, :], g, NT) - dd
        ds = (e.astype(jnp.float32) * dp).astype(jnp.bfloat16)
        dvt[:, at] += mm(glt, e, NT)
        dkt[:, at] += mm(qrt, ds, NT)
        return mm(kt[:, at], ds, NN)

    dqt = back(0, tile) + back(win, tile)
    dqt = lax.fori_loop(
        0, n_full // bk,
        lambda i, a: a + back(pl.multiple_of(tile + i * bk, tile), bk), dqt)
    dqt = dqt * rs
    for h in range(group):
        dq_ref[:, h * hd:(h + 1) * hd] = dqt[:, h * tile:(h + 1) * tile].T.astype(jnp.bfloat16)

    @pl.when(t == pl.num_programs(0) - 1)
    def _():
        for s in range(reach + 1):
            here = pl.ds(s * rows, rows)
            dk = dkt[:, here].T
            dv = dvt[:, here].T
            if s < reach:
                far_refs[s][:, :hd] = dk.astype(jnp.bfloat16)
                far_refs[s][:, hd:] = dv.astype(jnp.bfloat16)
            else:
                own_ref[:, :hd] = dk
                own_ref[:, hd:] = dv


def attention(queries, out_grad, skip, shards, slot, group, tile=256, bk=1920):
    hd = HEAD_DIM
    rows = queries.shape[0]
    reach = len(shards) - 1
    win = reach * rows
    total = win + rows
    cols = group * tile
    while (win - tile) % bk:
        bk -= tile
    whole = lambda shape: pl.BlockSpec(shape, lambda t: (0, 0), pipeline_mode=pl.Buffered(1))
    part = pl.BlockSpec((tile, group * hd), lambda t: (t, slot))
    outp = pl.BlockSpec((tile, group * hd), lambda t: (t, 0))
    area = win * rows * group
    return pl.pallas_call(
        functools.partial(attn_body, reach, tile, group, bk),
        out_shape=(
            jax.ShapeDtypeStruct((rows, group * hd), jnp.bfloat16),
            jax.ShapeDtypeStruct((rows, group * hd), jnp.bfloat16),
        ) + (jax.ShapeDtypeStruct((rows, 2 * hd), jnp.bfloat16),) * reach + (
            jax.ShapeDtypeStruct((rows, 2 * hd), jnp.float32),
        ),
        grid=(rows // tile,),
        in_specs=[pl.BlockSpec(memory_space=pltpu.SMEM), part, part] + [whole((rows, 2 * hd))] * (reach + 1),
        out_specs=(outp, outp) + (whole((rows, 2 * hd)),) * (reach + 1),
        scratch_shapes=[
            pltpu.VMEM((total, 2 * hd), jnp.bfloat16),
            pltpu.VMEM((total, hd), jnp.bfloat16),
            pltpu.VMEM((hd, total), jnp.bfloat16),
            pltpu.VMEM((hd + 16, total), jnp.bfloat16),
            pltpu.VMEM((win + tile, cols), jnp.float32),
            pltpu.VMEM((win + tile, cols), jnp.bfloat16),
            pltpu.VMEM((hd, total), jnp.float32),
            pltpu.VMEM((hd, total), jnp.float32),
        ],
        compiler_params=pltpu.CompilerParams(
            dimension_semantics=("arbitrary",), vmem_limit_bytes=60 << 20),
        cost_estimate=pl.CostEstimate(
            flops=12 * area * hd, bytes_accessed=16 << 20, transcendentals=area),
        name="window_attention",
    )(skip, queries, out_grad, *shards)


moment_decay = 0.8


def shifted(x, axis, by):
    length = lax.axis_size(axis)
    pairs = [(i, i + by) for i in range(length) if 0 <= i + by < length]
    return lax.ppermute(x, axis, pairs)


def after(value, *others):
    return lax.optimization_barrier((value,) + others)[0]


def row_split_refresh(grad_term_sum, moment, left_old, left_new, right_old, right_new):
    turn_share = lax.psum_scatter(
        jnp.einsum("brk,brj->kbj", right_old, right_new, preferred_element_type=jnp.float32),
        "seq", scatter_dimension=0, tiled=True)
    right_turn = jnp.transpose(turn_share, (1, 0, 2)).astype(jnp.bfloat16)
    turned = jnp.einsum(
        "brk,bkj->brj", moment, lax.all_gather(right_turn, "seq", axis=1, tiled=True),
        preferred_element_type=jnp.float32).astype(jnp.bfloat16)
    carried = jnp.einsum(
        "brk,bkj->brj", left_old, lax.all_gather(turned, "seq", axis=1, tiled=True),
        preferred_element_type=jnp.float32)
    grad_term = jnp.einsum(
        "brk,bkj->brj", grad_term_sum, lax.all_gather(right_new, "seq", axis=1, tiled=True),
        preferred_element_type=jnp.float32)
    inner = (moment_decay * carried + (1.0 - moment_decay) * grad_term).astype(jnp.bfloat16)
    new_share = lax.psum_scatter(
        jnp.einsum("brk,brj->kbj", left_new, inner, preferred_element_type=jnp.float32),
        "seq", scatter_dimension=0, tiled=True)
    return jnp.transpose(new_share, (1, 0, 2))


def bmm(spec, a, b):
    return jnp.einsum(spec, a, b, preferred_element_type=jnp.float32)


def project(columns, layer_input):
    return bmm("tj,tk->jk", columns, layer_input).astype(jnp.bfloat16)


def swap_sum(term, n, width):
    index = lax.axis_index("seq")
    if n & (n - 1):
        parts = jnp.stack([term[:, i * width:(i + 1) * width] for i in range(n)])
        return jnp.sum(lax.all_to_all(parts, "seq", 0, 0).astype(jnp.float32), axis=0)
    pieces = [lax.dynamic_slice_in_dim(term, 0, width, 1)] if n == 1 else None
    step = 1
    while step < n:
        mine = (index // step) % 2
        if pieces is None:
            starts = range(n // 2)
            keep = [lax.dynamic_slice_in_dim(term, (2 * i + mine) * width, width, 1) for i in starts]
            send = [lax.dynamic_slice_in_dim(term, (2 * i + 1 - mine) * width, width, 1) for i in starts]
            keep, send = jnp.stack(keep), jnp.stack(send)
        else:
            pairs = pieces.reshape((pieces.shape[0] // 2, 2) + pieces.shape[1:])
            keep = lax.dynamic_index_in_dim(pairs, mine, 1, False)
            send = lax.dynamic_index_in_dim(pairs, 1 - mine, 1, False).astype(jnp.bfloat16)
        got = lax.ppermute(send, "seq", [(i, i ^ step) for i in range(n)])
        pieces = keep.astype(jnp.float32) + got.astype(jnp.float32)
        step *= 2
    return pieces[0].astype(jnp.float32)


def per_device(
    queries, keys, values, out_grad, layer_input, moment, left_old, left_new, right_old, right_new
):
    n = lax.axis_size("seq")
    reach = n // 2
    seq_index = lax.axis_index("seq")
    rows = queries.shape[0]
    hd = HEAD_DIM
    kv_count = keys.shape[1] // hd
    group = queries.shape[1] // keys.shape[1]
    blocks, share_rows, order = moment.shape
    row_blocks = layer_input.shape[1] // order
    whole_blocks = row_blocks % n == 0 and (group + 2) * hd == order
    per_owner = row_blocks // n

    pairs = [
        jnp.concatenate([keys[:, k * hd:(k + 1) * hd], values[:, k * hd:(k + 1) * hd]], axis=1)
        for k in range(kv_count)
    ]
    skip = jnp.reshape(reach - seq_index, (1,)).astype(jnp.int32)

    windows = []
    gate = None
    for k in range(kv_count):
        held = pairs[k] if gate is None else after(pairs[k], gate)
        shards = [pairs[k]]
        if k == 0:
            for _ in range(reach):
                held = shifted(held, "seq", 1)
                shards.insert(0, held)
            gate = held
        else:
            for d in range(1, reach + 1):
                shards.insert(0, shifted(held, "seq", d))
        windows.append(shards)

    if whole_blocks:
        cut = [
            x.reshape(kv_count, n, per_owner, share_rows, order)
            for x in (moment, left_old, left_new, right_old, right_new)
        ]

        def message(owner):
            return jnp.stack([
                lax.dynamic_slice_in_dim(x, owner, 1, 1)[:, 0] for x in cut])

        whole = jnp.zeros((5, kv_count, per_owner, n, share_rows, order), jnp.bfloat16)
        whole = lax.dynamic_update_slice_in_dim(
            whole, message(seq_index)[:, :, :, None], seq_index, 3)
        leftward = []
        for d in range(1, n):
            packed = after(message((seq_index + n - d) % n), windows[0][reach - 1])
            leftward.append(shifted(packed, "seq", -d))
        rightward = []
    outs, query_grads, key_grads, value_grads, joined = [], [], [], [], []
    parts_sent = []
    for k in range(kv_count):
        last = k == kv_count - 1
        gate = after(skip, *leftward) if whole_blocks and k == 1 else skip
        head_out, head_dq, *grads = attention(queries, out_grad, gate, windows[k], k, group)
        far, own = grads[:reach], grads[reach]
        outs.append(head_out)
        query_grads.append(head_dq)
        if whole_blocks and k == 0:
            for d in range(1, n):
                packed = after(message((seq_index + d) % n), head_out)
                rightward.append(shifted(packed, "seq", d))
        if not last:
            for d in range(1, reach + 1):
                own = own + shifted(far[reach - d], "seq", -d).astype(jnp.float32)
        else:
            if whole_blocks:
                early = jnp.concatenate(joined + [head_dq], axis=1)
                early_term = swap_sum(project(early, layer_input), n, per_owner * order)
            carry = far[0]
            for d in range(reach, 0, -1):
                carry = shifted(carry, "seq", -1)
                if whole_blocks and d == reach:
                    carry = after(carry, *rightward)
                if d > 1:
                    carry = (carry.astype(jnp.float32) + far[reach - d + 1].astype(jnp.float32)).astype(jnp.bfloat16)
            if whole_blocks:
                for d in range(1, n):
                    source = (seq_index + d) % n
                    piece = jnp.where(seq_index + d < n, leftward[d - 1], rightward[n - d - 1])
                    whole = lax.dynamic_update_slice_in_dim(whole, piece[:, :, :, None], source, 3)
                m_own, lo_own, ln_own, ro_own, rn_own = whole.reshape(
                    5, kv_count, per_owner, order, order)
                right_turn = bmm("cbrk,cbrj->cbkj", ro_own, rn_own).astype(jnp.bfloat16)
                turned = bmm("cbrk,cbkj->cbrj", m_own, right_turn).astype(jnp.bfloat16)
                carried = moment_decay * bmm("cbrk,cbkj->cbrj", lo_own, turned)
                carry = after(carry, carried)
            own = own + carry.astype(jnp.float32)
        kv_grad = own.astype(jnp.bfloat16)
        key_grads.append(kv_grad[:, :hd])
        value_grads.append(kv_grad[:, hd:])
        joined.append(jnp.concatenate([head_dq, kv_grad], axis=1))
    if whole_blocks:
        late_term = swap_sum(project(kv_grad, layer_input), n, per_owner * order)
        grads = jnp.concatenate([early_term, late_term], axis=0).astype(jnp.bfloat16)
        news = []
        for k in range(kv_count):
            grad = grads[k * order:(k + 1) * order].reshape(order, per_owner, order)
            inner = carried[k] + (1.0 - moment_decay) * bmm("jbr,bjk->brk", grad, rn_own[k])
            new = bmm("brk,brj->bkj", ln_own[k], inner.astype(jnp.bfloat16)).astype(jnp.bfloat16)
            new = jnp.transpose(new.reshape(per_owner, n, share_rows, order), (1, 0, 2, 3))
            new = lax.all_to_all(new, "seq", 0, 0)
            news.append(new.reshape(row_blocks, share_rows, order).astype(jnp.float32))
    if whole_blocks:
        new_moment = jnp.concatenate(news, axis=0)
    else:
        joined = jnp.concatenate(joined, axis=1)
        term = bmm(
            "trk,tcj->kcrj",
            layer_input.reshape(rows, row_blocks, order),
            joined.reshape(rows, joined.shape[1] // order, order))
        share = lax.psum_scatter(
            term.reshape(order, blocks, order), "seq", scatter_dimension=0, tiled=True)
        new_moment = row_split_refresh(
            jnp.transpose(share, (1, 0, 2)).astype(jnp.bfloat16),
            moment, left_old, left_new, right_old, right_new)
    join = lambda parts: parts[0] if len(parts) == 1 else jnp.concatenate(parts, axis=1)
    return (join(outs), join(query_grads), join(key_grads), join(value_grads), new_moment)


def solution(mesh):
    both = P(("groups", "seq"), "grid")
    block = P(("groups", "grid"), "seq", None)
    return jax.shard_map(
        per_device,
        mesh=mesh,
        in_specs=(both, both, both, both, P(("groups", "seq"), None)) + (block,) * 5,
        out_specs=(both, both, both, both, block),
        check_vma=False,
    )
```

```python
import functools

import jax
import jax.numpy as jnp
from jax import lax
from jax.experimental import pallas as pl
from jax.experimental.pallas import tpu as pltpu
from jax.sharding import PartitionSpec as P

HEAD_DIM = 128
NEG = -1e30
LOG2E = 1.4426950408889634
NT = (((1,), (1,)), ((), ()))
NN = (((1,), (0,)), ((), ()))


def mm(a, b, dims):
    return lax.dot_general(a, b, dims, preferred_element_type=jnp.float32)


def attn_body(reach, tile, group, skip_ref, q_ref, g_ref, *rest):
    kv_refs = rest[: reach + 1]
    o_ref, dq_ref = rest[reach + 1: reach + 3]
    far_refs = rest[reach + 3: 2 * reach + 3]
    own_ref, kb, vb, kt, vt, s_buf, e_buf, dkt, dvt = rest[2 * reach + 3:]
    hd = HEAD_DIM
    t = pl.program_id(0)
    rows = kv_refs[0].shape[0]
    win = reach * rows
    cols = group * tile
    scale = hd ** -0.5

    @pl.when(t == 0)
    def _():
        first = lax.broadcasted_iota(jnp.int32, (rows, hd), 1) == 0
        for s, ref in enumerate(kv_refs):
            here = pl.ds(s * rows, rows)
            k = ref[:, :hd]
            v = ref[:, hd:]
            kb[here, :hd] = k
            hide = jnp.where(s < skip_ref[0], NEG, 0.0)
            kb[here, hd:] = jnp.where(first, hide, 0.0).astype(jnp.bfloat16)
            vb[here, :] = v
            kt[:, here] = k.T
            vt[:hd, here] = v.T
        vt[hd:, :] = jnp.ones((16, win + rows), jnp.bfloat16)
        dkt[...] = jnp.zeros_like(dkt)
        dvt[...] = jnp.zeros_like(dvt)

    q = jnp.concatenate([q_ref[:, h * hd:(h + 1) * hd] for h in range(group)], axis=0)
    g = jnp.concatenate([g_ref[:, h * hd:(h + 1) * hd] for h in range(group)], axis=0)
    lane = lax.broadcasted_iota(jnp.int32, (cols, hd), 1)
    qa = jnp.concatenate([q, jnp.where(lane == 0, 1.0, 0.0).astype(jnp.bfloat16)], axis=1)
    base = t * tile
    n_full = win - tile

    ki = lax.broadcasted_iota(jnp.int32, (tile, cols), 0)
    qi = lax.broadcasted_iota(jnp.int32, (tile, cols), 1) % tile

    def scores(off, size, keep=None):
        at = pl.ds(pl.multiple_of(base + off, tile), size)
        s = mm(kb[at, :], qa, NT)
        if keep is not None:
            s = jnp.where(keep, s, NEG)
        s_buf[pl.ds(off, size), :] = s
        return jnp.max(s.reshape(size // 8, 8, cols), axis=0)

    m8 = jnp.maximum(scores(0, tile, ki > qi), scores(win, tile, ki <= qi))
    m8 = jnp.maximum(m8, scores(tile, n_full))
    m = jnp.max(m8, axis=0, keepdims=True)
    mc = m * (scale * LOG2E)

    def weigh(off, size):
        at = pl.ds(pl.multiple_of(base + off, tile), size)
        e = jnp.exp2(s_buf[pl.ds(off, size), :] * (scale * LOG2E) - mc).astype(jnp.bfloat16)
        e_buf[pl.ds(off, size), :] = e
        return mm(vt[:, at], e, NN)

    ot = weigh(0, win + tile)
    rl = 1.0 / ot[hd:hd + 1, :]
    on = (ot[:hd, :] * rl).astype(jnp.bfloat16)
    on32 = on.astype(jnp.float32)
    gt = g.astype(jnp.float32).T
    qt = q.astype(jnp.float32).T
    dd = jnp.sum(gt * on32, axis=0, keepdims=True)
    for h in range(group):
        o_ref[:, h * hd:(h + 1) * hd] = on32[:, h * tile:(h + 1) * tile].T.astype(jnp.bfloat16)
    gl = (gt * rl).T.astype(jnp.bfloat16)
    rs = rl * scale
    qr = (qt * rs).T.astype(jnp.bfloat16)

    def back(off, size):
        at = pl.ds(pl.multiple_of(base + off, tile), size)
        e = e_buf[pl.ds(off, size), :]
        dp = mm(vb[at, :], g, NT) - dd
        ds = (e.astype(jnp.float32) * dp).astype(jnp.bfloat16)
        dvt[at, :] += mm(e, gl, NN)
        dkt[at, :] += mm(ds, qr, NN)
        return mm(kt[:, at], ds, NN)

    dqt = back(0, win + tile)
    dqt = dqt * rs
    for h in range(group):
        dq_ref[:, h * hd:(h + 1) * hd] = dqt[:, h * tile:(h + 1) * tile].T.astype(jnp.bfloat16)

    @pl.when(t == pl.num_programs(0) - 1)
    def _():
        for s in range(reach + 1):
            here = pl.ds(s * rows, rows)
            dk = dkt[here, :]
            dv = dvt[here, :]
            if s < reach:
                far_refs[s][:, :hd] = dk.astype(jnp.bfloat16)
                far_refs[s][:, hd:] = dv.astype(jnp.bfloat16)
            else:
                own_ref[:, :hd] = dk
                own_ref[:, hd:] = dv


def attention(queries, out_grad, skip, shards, slot, group, tile=256):
    hd = HEAD_DIM
    rows = queries.shape[0]
    reach = len(shards) - 1
    win = reach * rows
    total = win + rows
    cols = group * tile
    whole = lambda shape: pl.BlockSpec(shape, lambda t: (0, 0), pipeline_mode=pl.Buffered(1))
    part = pl.BlockSpec((tile, group * hd), lambda t: (t, slot))
    outp = pl.BlockSpec((tile, group * hd), lambda t: (t, 0))
    area = win * rows * group
    return pl.pallas_call(
        functools.partial(attn_body, reach, tile, group),
        out_shape=(
            jax.ShapeDtypeStruct((rows, group * hd), jnp.bfloat16),
            jax.ShapeDtypeStruct((rows, group * hd), jnp.bfloat16),
        ) + (jax.ShapeDtypeStruct((rows, 2 * hd), jnp.bfloat16),) * reach + (
            jax.ShapeDtypeStruct((rows, 2 * hd), jnp.float32),
        ),
        grid=(rows // tile,),
        in_specs=[pl.BlockSpec(memory_space=pltpu.SMEM), part, part] + [whole((rows, 2 * hd))] * (reach + 1),
        out_specs=(outp, outp) + (whole((rows, 2 * hd)),) * (reach + 1),
        scratch_shapes=[
            pltpu.VMEM((total, 2 * hd), jnp.bfloat16),
            pltpu.VMEM((total, hd), jnp.bfloat16),
            pltpu.VMEM((hd, total), jnp.bfloat16),
            pltpu.VMEM((hd + 16, total), jnp.bfloat16),
            pltpu.VMEM((win + tile, cols), jnp.float32),
            pltpu.VMEM((win + tile, cols), jnp.bfloat16),
            pltpu.VMEM((total, hd), jnp.float32),
            pltpu.VMEM((total, hd), jnp.float32),
        ],
        compiler_params=pltpu.CompilerParams(
            dimension_semantics=("arbitrary",), vmem_limit_bytes=60 << 20),
        cost_estimate=pl.CostEstimate(
            flops=12 * area * hd, bytes_accessed=16 << 20, transcendentals=area),
        name="window_attention",
    )(skip, queries, out_grad, *shards)


moment_decay = 0.8


def shifted(x, axis, by, first=0):
    length = lax.axis_size(axis)
    pairs = [(i, i + by) for i in range(first, length) if 0 <= i + by < length]
    return lax.ppermute(x, axis, pairs)


def after(value, *others):
    return lax.optimization_barrier((value,) + others)[0]


def row_split_refresh(grad_term_sum, moment, left_old, left_new, right_old, right_new):
    turn_share = lax.psum_scatter(
        jnp.einsum("brk,brj->kbj", right_old, right_new, preferred_element_type=jnp.float32),
        "seq", scatter_dimension=0, tiled=True)
    right_turn = jnp.transpose(turn_share, (1, 0, 2)).astype(jnp.bfloat16)
    turned = jnp.einsum(
        "brk,bkj->brj", moment, lax.all_gather(right_turn, "seq", axis=1, tiled=True),
        preferred_element_type=jnp.float32).astype(jnp.bfloat16)
    carried = jnp.einsum(
        "brk,bkj->brj", left_old, lax.all_gather(turned, "seq", axis=1, tiled=True),
        preferred_element_type=jnp.float32)
    grad_term = jnp.einsum(
        "brk,bkj->brj", grad_term_sum, lax.all_gather(right_new, "seq", axis=1, tiled=True),
        preferred_element_type=jnp.float32)
    inner = (moment_decay * carried + (1.0 - moment_decay) * grad_term).astype(jnp.bfloat16)
    new_share = lax.psum_scatter(
        jnp.einsum("brk,brj->kbj", left_new, inner, preferred_element_type=jnp.float32),
        "seq", scatter_dimension=0, tiled=True)
    return jnp.transpose(new_share, (1, 0, 2))


def bmm(spec, a, b):
    return jnp.einsum(spec, a, b, preferred_element_type=jnp.float32)


def project(columns, layer_input):
    return bmm("tj,tk->jk", columns, layer_input).astype(jnp.bfloat16)


def swap_sum(term, n, width):
    index = lax.axis_index("seq")
    if n & (n - 1):
        parts = jnp.stack([term[:, i * width:(i + 1) * width] for i in range(n)])
        return jnp.sum(lax.all_to_all(parts, "seq", 0, 0).astype(jnp.float32), axis=0)
    pieces = [lax.dynamic_slice_in_dim(term, 0, width, 1)] if n == 1 else None
    step = 1
    while step < n:
        mine = (index // step) % 2
        if pieces is None:
            starts = range(n // 2)
            keep = [lax.dynamic_slice_in_dim(term, (2 * i + mine) * width, width, 1) for i in starts]
            send = [lax.dynamic_slice_in_dim(term, (2 * i + 1 - mine) * width, width, 1) for i in starts]
            keep, send = jnp.stack(keep), jnp.stack(send)
        else:
            pairs = pieces.reshape((pieces.shape[0] // 2, 2) + pieces.shape[1:])
            keep = lax.dynamic_index_in_dim(pairs, mine, 1, False)
            send = lax.dynamic_index_in_dim(pairs, 1 - mine, 1, False).astype(jnp.bfloat16)
        got = lax.ppermute(send, "seq", [(i, i ^ step) for i in range(n)])
        pieces = keep.astype(jnp.float32) + got.astype(jnp.float32)
        step *= 2
    return pieces[0].astype(jnp.float32)


def per_device(
    queries, keys, values, out_grad, layer_input, moment, left_old, left_new, right_old, right_new
):
    n = lax.axis_size("seq")
    reach = n // 2
    seq_index = lax.axis_index("seq")
    rows = queries.shape[0]
    hd = HEAD_DIM
    kv_count = keys.shape[1] // hd
    group = queries.shape[1] // keys.shape[1]
    blocks, share_rows, order = moment.shape
    row_blocks = layer_input.shape[1] // order
    whole_blocks = row_blocks % n == 0 and (group + 2) * hd == order
    per_owner = row_blocks // n

    pairs = [
        jnp.concatenate([keys[:, k * hd:(k + 1) * hd], values[:, k * hd:(k + 1) * hd]], axis=1)
        for k in range(kv_count)
    ]
    skip = jnp.reshape(reach - seq_index, (1,)).astype(jnp.int32)

    windows = []
    gate = None
    for k in range(kv_count):
        held = pairs[k] if gate is None else after(pairs[k], gate)
        shards = [pairs[k]]
        if k == 0:
            for hop in range(reach):
                held = shifted(held, "seq", 1, hop)
                shards.insert(0, held)
            gate = held
        else:
            for d in range(1, reach + 1):
                shards.insert(0, shifted(held, "seq", d))
        windows.append(shards)

    if whole_blocks:
        cut = [
            x.reshape(kv_count, n, per_owner, share_rows, order)
            for x in (moment, left_old, left_new, right_old, right_new)
        ]

        def message(owner):
            return jnp.stack([
                lax.dynamic_slice_in_dim(x, owner, 1, 1)[:, 0] for x in cut])

        whole = jnp.zeros((5, kv_count, per_owner, n, share_rows, order), jnp.bfloat16)
        whole = lax.dynamic_update_slice_in_dim(
            whole, message(seq_index)[:, :, :, None], seq_index, 3)
        leftward = []
        for d in range(1, n):
            packed = message((seq_index + n - d) % n)
            if d > 1:
                packed = after(packed, windows[0][reach - 1])
            leftward.append(shifted(packed, "seq", -d))
        rightward = []
    outs, query_grads, key_grads, value_grads, joined = [], [], [], [], []
    parts_sent = []
    for k in range(kv_count):
        last = k == kv_count - 1
        gate = after(skip, *leftward) if whole_blocks and k == 1 else skip
        head_out, head_dq, *grads = attention(queries, out_grad, gate, windows[k], k, group)
        far, own = grads[:reach], grads[reach]
        outs.append(head_out)
        query_grads.append(head_dq)
        if whole_blocks and k == 0:
            for d in range(1, n):
                packed = after(message((seq_index + d) % n), head_out)
                rightward.append(shifted(packed, "seq", d))
        if not last:
            for d in range(1, reach + 1):
                own = own + shifted(far[reach - d], "seq", -d).astype(jnp.float32)
        else:
            if whole_blocks:
                early = jnp.concatenate(joined + [head_dq], axis=1)
                early_term = swap_sum(project(early, layer_input), n, per_owner * order)
            carry = far[0]
            for d in range(reach, 0, -1):
                carry = shifted(carry, "seq", -1, d)
                if whole_blocks and d == reach:
                    whole = after(whole, carry)
                if d > 1:
                    carry = (carry.astype(jnp.float32) + far[reach - d + 1].astype(jnp.float32)).astype(jnp.bfloat16)
            if whole_blocks:
                for d in range(1, n):
                    source = (seq_index + d) % n
                    piece = jnp.where(seq_index + d < n, leftward[d - 1], rightward[n - d - 1])
                    whole = lax.dynamic_update_slice_in_dim(whole, piece[:, :, :, None], source, 3)
                m_own, lo_own, ln_own, ro_own, rn_own = whole.reshape(
                    5, kv_count, per_owner, order, order)
                right_turn = bmm("cbrk,cbrj->cbkj", ro_own, rn_own).astype(jnp.bfloat16)
                turned = bmm("cbrk,cbkj->cbrj", m_own, right_turn).astype(jnp.bfloat16)
                carried = moment_decay * bmm("cbrk,cbkj->cbrj", lo_own, turned)
                carry = after(carry, carried)
            own = own + carry.astype(jnp.float32)
        kv_grad = own.astype(jnp.bfloat16)
        key_grads.append(kv_grad[:, :hd])
        value_grads.append(kv_grad[:, hd:])
        joined.append(jnp.concatenate([head_dq, kv_grad], axis=1))
    if whole_blocks:
        late_term = swap_sum(project(kv_grad, layer_input), n, per_owner * order)
        grads = jnp.concatenate([early_term, late_term], axis=0).astype(jnp.bfloat16)
        news = []
        for k in range(kv_count):
            grad = grads[k * order:(k + 1) * order].reshape(order, per_owner, order)
            inner = carried[k] + (1.0 - moment_decay) * bmm("jbr,bjk->brk", grad, rn_own[k])
            new = bmm("brk,brj->bkj", ln_own[k], inner.astype(jnp.bfloat16)).astype(jnp.bfloat16)
            new = jnp.transpose(new.reshape(per_owner, n, share_rows, order), (1, 0, 2, 3))
            new = lax.all_to_all(new, "seq", 0, 0)
            news.append(new.reshape(row_blocks, share_rows, order).astype(jnp.float32))
    if whole_blocks:
        new_moment = jnp.concatenate(news, axis=0)
    else:
        joined = jnp.concatenate(joined, axis=1)
        term = bmm(
            "trk,tcj->kcrj",
            layer_input.reshape(rows, row_blocks, order),
            joined.reshape(rows, joined.shape[1] // order, order))
        share = lax.psum_scatter(
            term.reshape(order, blocks, order), "seq", scatter_dimension=0, tiled=True)
        new_moment = row_split_refresh(
            jnp.transpose(share, (1, 0, 2)).astype(jnp.bfloat16),
            moment, left_old, left_new, right_old, right_new)
    join = lambda parts: parts[0] if len(parts) == 1 else jnp.concatenate(parts, axis=1)
    return (join(outs), join(query_grads), join(key_grads), join(value_grads), new_moment)


def solution(mesh):
    both = P(("groups", "seq"), "grid")
    block = P(("groups", "grid"), "seq", None)
    return jax.shard_map(
        per_device,
        mesh=mesh,
        in_specs=(both, both, both, both, P(("groups", "seq"), None)) + (block,) * 5,
        out_specs=(both, both, both, both, block),
        check_vma=False,
    )
```

```python
import functools

import jax
import jax.numpy as jnp
from jax import lax
from jax.experimental import pallas as pl
from jax.experimental.pallas import tpu as pltpu
from jax.sharding import PartitionSpec as P

HEAD_DIM = 128
NEG = -1e30
LOG2E = 1.4426950408889634
NT = (((1,), (1,)), ((), ()))
NN = (((1,), (0,)), ((), ()))


def mm(a, b, dims):
    return lax.dot_general(a, b, dims, preferred_element_type=jnp.float32)


def attn_body(reach, tile, group, skip_ref, q_ref, g_ref, *rest):
    kv_refs = rest[: reach + 1]
    o_ref, dq_ref = rest[reach + 1: reach + 3]
    far_refs = rest[reach + 3: 2 * reach + 3]
    own_ref, kb, vb, kt, vt, s_buf, e_buf, dkt, dvt = rest[2 * reach + 3:]
    hd = HEAD_DIM
    t = pl.program_id(0)
    rows = kv_refs[0].shape[0]
    win = reach * rows
    cols = group * tile
    scale = hd ** -0.5

    @pl.when(t == 0)
    def _():
        first = lax.broadcasted_iota(jnp.int32, (rows, hd), 1) == 0
        for s, ref in enumerate(kv_refs):
            here = pl.ds(s * rows, rows)
            k = ref[:, :hd]
            v = ref[:, hd:]
            kb[here, :hd] = k
            hide = jnp.where(s < skip_ref[0], NEG, 0.0)
            kb[here, hd:] = jnp.where(first, hide, 0.0).astype(jnp.bfloat16)
            vb[here, :] = v
            kt[:, here] = k.T
            vt[:hd, here] = v.T
        vt[hd:, :] = jnp.ones((16, win + rows), jnp.bfloat16)
        dkt[...] = jnp.zeros_like(dkt)
        dvt[...] = jnp.zeros_like(dvt)

    q = jnp.concatenate([q_ref[:, h * hd:(h + 1) * hd] for h in range(group)], axis=0)
    g = jnp.concatenate([g_ref[:, h * hd:(h + 1) * hd] for h in range(group)], axis=0)
    lane = lax.broadcasted_iota(jnp.int32, (cols, hd), 1)
    qa = jnp.concatenate([q, jnp.where(lane == 0, 1.0, 0.0).astype(jnp.bfloat16)], axis=1)
    base = t * tile
    n_full = win - tile

    ki = lax.broadcasted_iota(jnp.int32, (tile, cols), 0)
    qi = lax.broadcasted_iota(jnp.int32, (tile, cols), 1) % tile

    def scores(off, size, keep=None):
        at = pl.ds(pl.multiple_of(base + off, tile), size)
        s = mm(kb[at, :], qa, NT)
        if keep is not None:
            s = jnp.where(keep, s, NEG)
        s_buf[pl.ds(off, size), :] = s
        return jnp.max(s.reshape(size // 8, 8, cols), axis=0)

    m8 = jnp.maximum(scores(0, tile, ki > qi), scores(win, tile, ki <= qi))
    m8 = jnp.maximum(m8, scores(tile, n_full))
    m = jnp.max(m8, axis=0, keepdims=True)
    mc = m * (scale * LOG2E)

    def weigh(off, size):
        at = pl.ds(pl.multiple_of(base + off, tile), size)
        e = jnp.exp2(s_buf[pl.ds(off, size), :] * (scale * LOG2E) - mc).astype(jnp.bfloat16)
        e_buf[pl.ds(off, size), :] = e
        return mm(vt[:, at], e, NN)

    ot = weigh(0, win + tile)
    rl = 1.0 / ot[hd:hd + 1, :]
    on = (ot[:hd, :] * rl).astype(jnp.bfloat16)
    on32 = on.astype(jnp.float32)
    gt = g.astype(jnp.float32).T
    qt = q.astype(jnp.float32).T
    dd = jnp.sum(gt * on32, axis=0, keepdims=True)
    for h in range(group):
        o_ref[:, h * hd:(h + 1) * hd] = on32[:, h * tile:(h + 1) * tile].T.astype(jnp.bfloat16)
    gl = (gt * rl).T.astype(jnp.bfloat16)
    rs = rl * scale
    qr = (qt * rs).T.astype(jnp.bfloat16)

    def back(off, size):
        at = pl.ds(pl.multiple_of(base + off, tile), size)
        e = e_buf[pl.ds(off, size), :]
        dp = mm(vb[at, :], g, NT) - dd
        ds = (e.astype(jnp.float32) * dp).astype(jnp.bfloat16)
        dvt[at, :] += mm(e, gl, NN)
        dkt[at, :] += mm(ds, qr, NN)
        return mm(kt[:, at], ds, NN)

    dqt = back(0, win + tile)
    dqt = dqt * rs
    for h in range(group):
        dq_ref[:, h * hd:(h + 1) * hd] = dqt[:, h * tile:(h + 1) * tile].T.astype(jnp.bfloat16)

    @pl.when(t == pl.num_programs(0) - 1)
    def _():
        for s in range(reach + 1):
            here = pl.ds(s * rows, rows)
            dk = dkt[here, :]
            dv = dvt[here, :]
            if s < reach:
                far_refs[s][:, :hd] = dk.astype(jnp.bfloat16)
                far_refs[s][:, hd:] = dv.astype(jnp.bfloat16)
            else:
                own_ref[:, :hd] = dk
                own_ref[:, hd:] = dv


def attention(queries, out_grad, skip, shards, slot, group, tile=256):
    hd = HEAD_DIM
    rows = queries.shape[0]
    reach = len(shards) - 1
    win = reach * rows
    total = win + rows
    cols = group * tile
    whole = lambda shape: pl.BlockSpec(shape, lambda t: (0, 0), pipeline_mode=pl.Buffered(1))
    part = pl.BlockSpec((tile, group * hd), lambda t: (t, slot))
    outp = pl.BlockSpec((tile, group * hd), lambda t: (t, 0))
    area = win * rows * group
    return pl.pallas_call(
        functools.partial(attn_body, reach, tile, group),
        out_shape=(
            jax.ShapeDtypeStruct((rows, group * hd), jnp.bfloat16),
            jax.ShapeDtypeStruct((rows, group * hd), jnp.bfloat16),
        ) + (jax.ShapeDtypeStruct((rows, 2 * hd), jnp.bfloat16),) * reach + (
            jax.ShapeDtypeStruct((rows, 2 * hd), jnp.float32),
        ),
        grid=(rows // tile,),
        in_specs=[pl.BlockSpec(memory_space=pltpu.SMEM), part, part] + [whole((rows, 2 * hd))] * (reach + 1),
        out_specs=(outp, outp) + (whole((rows, 2 * hd)),) * (reach + 1),
        scratch_shapes=[
            pltpu.VMEM((total, 2 * hd), jnp.bfloat16),
            pltpu.VMEM((total, hd), jnp.bfloat16),
            pltpu.VMEM((hd, total), jnp.bfloat16),
            pltpu.VMEM((hd + 16, total), jnp.bfloat16),
            pltpu.VMEM((win + tile, cols), jnp.float32),
            pltpu.VMEM((win + tile, cols), jnp.bfloat16),
            pltpu.VMEM((total, hd), jnp.float32),
            pltpu.VMEM((total, hd), jnp.float32),
        ],
        compiler_params=pltpu.CompilerParams(
            dimension_semantics=("arbitrary",), vmem_limit_bytes=60 << 20),
        cost_estimate=pl.CostEstimate(
            flops=12 * area * hd, bytes_accessed=16 << 20, transcendentals=area),
        name="window_attention",
    )(skip, queries, out_grad, *shards)


moment_decay = 0.8


def shifted(x, axis, by, first=0):
    length = lax.axis_size(axis)
    pairs = [(i, i + by) for i in range(first, length) if 0 <= i + by < length]
    return lax.ppermute(x, axis, pairs)


def after(value, *others):
    return lax.optimization_barrier((value,) + others)[0]


def row_split_refresh(grad_term_sum, moment, left_old, left_new, right_old, right_new):
    turn_share = lax.psum_scatter(
        jnp.einsum("brk,brj->kbj", right_old, right_new, preferred_element_type=jnp.float32),
        "seq", scatter_dimension=0, tiled=True)
    right_turn = jnp.transpose(turn_share, (1, 0, 2)).astype(jnp.bfloat16)
    turned = jnp.einsum(
        "brk,bkj->brj", moment, lax.all_gather(right_turn, "seq", axis=1, tiled=True),
        preferred_element_type=jnp.float32).astype(jnp.bfloat16)
    carried = jnp.einsum(
        "brk,bkj->brj", left_old, lax.all_gather(turned, "seq", axis=1, tiled=True),
        preferred_element_type=jnp.float32)
    grad_term = jnp.einsum(
        "brk,bkj->brj", grad_term_sum, lax.all_gather(right_new, "seq", axis=1, tiled=True),
        preferred_element_type=jnp.float32)
    inner = (moment_decay * carried + (1.0 - moment_decay) * grad_term).astype(jnp.bfloat16)
    new_share = lax.psum_scatter(
        jnp.einsum("brk,brj->kbj", left_new, inner, preferred_element_type=jnp.float32),
        "seq", scatter_dimension=0, tiled=True)
    return jnp.transpose(new_share, (1, 0, 2))


def bmm(spec, a, b):
    return jnp.einsum(spec, a, b, preferred_element_type=jnp.float32)


def project(columns, layer_input):
    return bmm("tj,tk->jk", columns, layer_input).astype(jnp.bfloat16)


def swap_sum(term, n, width):
    index = lax.axis_index("seq")
    if n & (n - 1):
        parts = jnp.stack([term[:, i * width:(i + 1) * width] for i in range(n)])
        return jnp.sum(lax.all_to_all(parts, "seq", 0, 0).astype(jnp.float32), axis=0)
    pieces = [lax.dynamic_slice_in_dim(term, 0, width, 1)] if n == 1 else None
    step = 1
    while step < n:
        mine = (index // step) % 2
        if pieces is None:
            starts = range(n // 2)
            keep = [lax.dynamic_slice_in_dim(term, (2 * i + mine) * width, width, 1) for i in starts]
            send = [lax.dynamic_slice_in_dim(term, (2 * i + 1 - mine) * width, width, 1) for i in starts]
            keep, send = jnp.stack(keep), jnp.stack(send)
        else:
            pairs = pieces.reshape((pieces.shape[0] // 2, 2) + pieces.shape[1:])
            keep = lax.dynamic_index_in_dim(pairs, mine, 1, False)
            send = lax.dynamic_index_in_dim(pairs, 1 - mine, 1, False).astype(jnp.bfloat16)
        got = lax.ppermute(send, "seq", [(i, i ^ step) for i in range(n)])
        pieces = keep.astype(jnp.float32) + got.astype(jnp.float32)
        step *= 2
    return pieces[0].astype(jnp.float32)


def per_device(
    queries, keys, values, out_grad, layer_input, moment, left_old, left_new, right_old, right_new
):
    n = lax.axis_size("seq")
    reach = n // 2
    seq_index = lax.axis_index("seq")
    rows = queries.shape[0]
    hd = HEAD_DIM
    kv_count = keys.shape[1] // hd
    group = queries.shape[1] // keys.shape[1]
    blocks, share_rows, order = moment.shape
    row_blocks = layer_input.shape[1] // order
    whole_blocks = row_blocks % n == 0 and (group + 2) * hd == order
    per_owner = row_blocks // n

    pairs = [
        jnp.concatenate([keys[:, k * hd:(k + 1) * hd], values[:, k * hd:(k + 1) * hd]], axis=1)
        for k in range(kv_count)
    ]
    skip = jnp.reshape(reach - seq_index, (1,)).astype(jnp.int32)

    windows = []
    gate = None
    for k in range(kv_count):
        held = pairs[k] if gate is None else after(pairs[k], gate)
        shards = [pairs[k]]
        if k == 0:
            for hop in range(reach):
                held = shifted(held, "seq", 1, hop)
                shards.insert(0, held)
            gate = held
        else:
            for d in range(1, reach + 1):
                shards.insert(0, shifted(held, "seq", d))
        windows.append(shards)

    if whole_blocks:
        cut = [
            x.reshape(kv_count, n, per_owner, share_rows, order)
            for x in (moment, left_old, left_new, right_old, right_new)
        ]

        def message(owner):
            return jnp.stack([
                lax.dynamic_slice_in_dim(x, owner, 1, 1)[:, 0] for x in cut])

        whole = jnp.zeros((5, kv_count, per_owner, n, share_rows, order), jnp.bfloat16)
        whole = lax.dynamic_update_slice_in_dim(
            whole, message(seq_index)[:, :, :, None], seq_index, 3)
        leftward = []
        for d in range(1, n):
            packed = message((seq_index + n - d) % n)
            if d > 1:
                packed = after(packed, windows[0][reach - 1])
            leftward.append(shifted(packed, "seq", -d))
        rightward = []
    outs, query_grads, key_grads, value_grads, joined = [], [], [], [], []
    parts_sent = []
    for k in range(kv_count):
        last = k == kv_count - 1
        gate = skip
        if whole_blocks and k < 2:
            gate = after(skip, *(leftward[1:] if k else leftward[:1]))
        head_out, head_dq, *grads = attention(queries, out_grad, gate, windows[k], k, group)
        far, own = grads[:reach], grads[reach]
        outs.append(head_out)
        query_grads.append(head_dq)
        if whole_blocks and k == 0:
            for d in range(1, n):
                packed = after(message((seq_index + d) % n), head_out)
                rightward.append(shifted(packed, "seq", d))
        if not last:
            for d in range(1, reach + 1):
                own = own + shifted(far[reach - d], "seq", -d).astype(jnp.float32)
        else:
            if whole_blocks:
                early = jnp.concatenate(joined + [head_dq], axis=1)
                early_term = swap_sum(project(early, layer_input), n, per_owner * order)
            carry = far[0]
            for d in range(reach, 0, -1):
                carry = shifted(carry, "seq", -1, d)
                if whole_blocks and d == reach:
                    whole = after(whole, carry)
                if d > 1:
                    carry = (carry.astype(jnp.float32) + far[reach - d + 1].astype(jnp.float32)).astype(jnp.bfloat16)
            if whole_blocks:
                for d in range(1, n):
                    source = (seq_index + d) % n
                    piece = jnp.where(seq_index + d < n, leftward[d - 1], rightward[n - d - 1])
                    whole = lax.dynamic_update_slice_in_dim(whole, piece[:, :, :, None], source, 3)
                m_own, lo_own, ln_own, ro_own, rn_own = whole.reshape(
                    5, kv_count, per_owner, order, order)
                right_turn = bmm("cbrk,cbrj->cbkj", ro_own, rn_own).astype(jnp.bfloat16)
                turned = bmm("cbrk,cbkj->cbrj", m_own, right_turn).astype(jnp.bfloat16)
                carried = moment_decay * bmm("cbrk,cbkj->cbrj", lo_own, turned)
                carry = after(carry, carried)
            own = own + carry.astype(jnp.float32)
        kv_grad = own.astype(jnp.bfloat16)
        key_grads.append(kv_grad[:, :hd])
        value_grads.append(kv_grad[:, hd:])
        joined.append(jnp.concatenate([head_dq, kv_grad], axis=1))
    if whole_blocks:
        late_term = swap_sum(project(kv_grad, layer_input), n, per_owner * order)
        grads = jnp.concatenate([early_term, late_term], axis=0).astype(jnp.bfloat16)
        news = []
        for k in range(kv_count):
            grad = grads[k * order:(k + 1) * order].reshape(order, per_owner, order)
            inner = carried[k] + (1.0 - moment_decay) * bmm("jbr,bjk->brk", grad, rn_own[k])
            new = bmm("brk,brj->bkj", ln_own[k], inner.astype(jnp.bfloat16)).astype(jnp.bfloat16)
            new = jnp.transpose(new.reshape(per_owner, n, share_rows, order), (1, 0, 2, 3))
            new = lax.all_to_all(new, "seq", 0, 0)
            news.append(new.reshape(row_blocks, share_rows, order).astype(jnp.float32))
    if whole_blocks:
        new_moment = jnp.concatenate(news, axis=0)
    else:
        joined = jnp.concatenate(joined, axis=1)
        term = bmm(
            "trk,tcj->kcrj",
            layer_input.reshape(rows, row_blocks, order),
            joined.reshape(rows, joined.shape[1] // order, order))
        share = lax.psum_scatter(
            term.reshape(order, blocks, order), "seq", scatter_dimension=0, tiled=True)
        new_moment = row_split_refresh(
            jnp.transpose(share, (1, 0, 2)).astype(jnp.bfloat16),
            moment, left_old, left_new, right_old, right_new)
    join = lambda parts: parts[0] if len(parts) == 1 else jnp.concatenate(parts, axis=1)
    return (join(outs), join(query_grads), join(key_grads), join(value_grads), new_moment)


def solution(mesh):
    both = P(("groups", "seq"), "grid")
    block = P(("groups", "grid"), "seq", None)
    return jax.shard_map(
        per_device,
        mesh=mesh,
        in_specs=(both, both, both, both, P(("groups", "seq"), None)) + (block,) * 5,
        out_specs=(both, both, both, both, block),
        check_vma=False,
    )
```

```python
import functools

import jax
import jax.numpy as jnp
from jax import lax
from jax.experimental import pallas as pl
from jax.experimental.pallas import tpu as pltpu
from jax.sharding import PartitionSpec as P

HEAD_DIM = 128
NEG = -1e30
LOG2E = 1.4426950408889634
NT = (((1,), (1,)), ((), ()))
NN = (((1,), (0,)), ((), ()))


def mm(a, b, dims):
    return lax.dot_general(a, b, dims, preferred_element_type=jnp.float32)


def attn_body(reach, tile, group, skip_ref, q_ref, g_ref, *rest):
    kv_refs = rest[: reach + 1]
    o_ref, dq_ref = rest[reach + 1: reach + 3]
    far_refs = rest[reach + 3: 2 * reach + 3]
    own_ref, kb, vb, kt, vt, s_buf, e_buf, dkt, dvt = rest[2 * reach + 3:]
    hd = HEAD_DIM
    t = pl.program_id(0)
    rows = kv_refs[0].shape[0]
    win = reach * rows
    cols = group * tile
    scale = hd ** -0.5

    @pl.when(t == 0)
    def _():
        first = lax.broadcasted_iota(jnp.int32, (rows, hd), 1) == 0
        for s, ref in enumerate(kv_refs):
            here = pl.ds(s * rows, rows)
            k = ref[:, :hd]
            v = ref[:, hd:]
            kb[here, :hd] = k
            hide = jnp.where(s < skip_ref[0], NEG, 0.0)
            kb[here, hd:] = jnp.where(first, hide, 0.0).astype(jnp.bfloat16)
            vb[here, :] = v
            kt[:, here] = k.T
            vt[:hd, here] = v.T
        vt[hd:, :] = jnp.ones((16, win + rows), jnp.bfloat16)
        dkt[...] = jnp.zeros_like(dkt)
        dvt[...] = jnp.zeros_like(dvt)

    q = jnp.concatenate([q_ref[:, h * hd:(h + 1) * hd] for h in range(group)], axis=0)
    g = jnp.concatenate([g_ref[:, h * hd:(h + 1) * hd] for h in range(group)], axis=0)
    lane = lax.broadcasted_iota(jnp.int32, (cols, hd), 1)
    qa = jnp.concatenate([q, jnp.where(lane == 0, 1.0, 0.0).astype(jnp.bfloat16)], axis=1)
    base = t * tile
    n_full = win - tile

    ki = lax.broadcasted_iota(jnp.int32, (tile, cols), 0)
    qi = lax.broadcasted_iota(jnp.int32, (tile, cols), 1) % tile

    def scores(off, size, keep=None):
        at = pl.ds(pl.multiple_of(base + off, tile), size)
        s = mm(kb[at, :], qa, NT)
        if keep is not None:
            s = jnp.where(keep, s, NEG)
        s_buf[pl.ds(off, size), :] = s
        return jnp.max(s.reshape(size // 8, 8, cols), axis=0)

    m8 = jnp.maximum(scores(0, tile, ki > qi), scores(win, tile, ki <= qi))
    m8 = jnp.maximum(m8, scores(tile, n_full))
    m = jnp.max(m8, axis=0, keepdims=True)
    mc = m * (scale * LOG2E)

    def weigh(off, size):
        at = pl.ds(pl.multiple_of(base + off, tile), size)
        e = jnp.exp2(s_buf[pl.ds(off, size), :] * (scale * LOG2E) - mc).astype(jnp.bfloat16)
        e_buf[pl.ds(off, size), :] = e
        return mm(vt[:, at], e, NN)

    ot = weigh(0, win + tile)
    rl = 1.0 / ot[hd:hd + 1, :]
    on = (ot[:hd, :] * rl).astype(jnp.bfloat16)
    on32 = on.astype(jnp.float32)
    gt = g.astype(jnp.float32).T
    qt = q.astype(jnp.float32).T
    dd = jnp.sum(gt * on32, axis=0, keepdims=True)
    for h in range(group):
        o_ref[:, h * hd:(h + 1) * hd] = on32[:, h * tile:(h + 1) * tile].T.astype(jnp.bfloat16)
    gl = (gt * rl).T.astype(jnp.bfloat16)
    rs = rl * scale
    qr = (qt * rs).T.astype(jnp.bfloat16)

    def back(off, size):
        at = pl.ds(pl.multiple_of(base + off, tile), size)
        e = e_buf[pl.ds(off, size), :]
        dp = mm(vb[at, :], g, NT) - dd
        ds = (e.astype(jnp.float32) * dp).astype(jnp.bfloat16)
        dvt[at, :] += mm(e, gl, NN)
        dkt[at, :] += mm(ds, qr, NN)
        return mm(kt[:, at], ds, NN)

    dqt = back(0, win + tile)
    dqt = dqt * rs
    for h in range(group):
        dq_ref[:, h * hd:(h + 1) * hd] = dqt[:, h * tile:(h + 1) * tile].T.astype(jnp.bfloat16)

    @pl.when(t == pl.num_programs(0) - 1)
    def _():
        for s in range(reach + 1):
            here = pl.ds(s * rows, rows)
            dk = dkt[here, :]
            dv = dvt[here, :]
            if s < reach:
                far_refs[s][:, :hd] = dk.astype(jnp.bfloat16)
                far_refs[s][:, hd:] = dv.astype(jnp.bfloat16)
            else:
                own_ref[:, :hd] = dk
                own_ref[:, hd:] = dv


def attention(queries, out_grad, skip, shards, slot, group, tile=256):
    hd = HEAD_DIM
    rows = queries.shape[0]
    reach = len(shards) - 1
    win = reach * rows
    total = win + rows
    cols = group * tile
    whole = lambda shape: pl.BlockSpec(shape, lambda t: (0, 0), pipeline_mode=pl.Buffered(1))
    part = pl.BlockSpec((tile, group * hd), lambda t: (t, slot))
    outp = pl.BlockSpec((tile, group * hd), lambda t: (t, 0))
    area = win * rows * group
    return pl.pallas_call(
        functools.partial(attn_body, reach, tile, group),
        out_shape=(
            jax.ShapeDtypeStruct((rows, group * hd), jnp.bfloat16),
            jax.ShapeDtypeStruct((rows, group * hd), jnp.bfloat16),
        ) + (jax.ShapeDtypeStruct((rows, 2 * hd), jnp.bfloat16),) * reach + (
            jax.ShapeDtypeStruct((rows, 2 * hd), jnp.float32),
        ),
        grid=(rows // tile,),
        in_specs=[pl.BlockSpec(memory_space=pltpu.SMEM), part, part] + [whole((rows, 2 * hd))] * (reach + 1),
        out_specs=(outp, outp) + (whole((rows, 2 * hd)),) * (reach + 1),
        scratch_shapes=[
            pltpu.VMEM((total, 2 * hd), jnp.bfloat16),
            pltpu.VMEM((total, hd), jnp.bfloat16),
            pltpu.VMEM((hd, total), jnp.bfloat16),
            pltpu.VMEM((hd + 16, total), jnp.bfloat16),
            pltpu.VMEM((win + tile, cols), jnp.float32),
            pltpu.VMEM((win + tile, cols), jnp.bfloat16),
            pltpu.VMEM((total, hd), jnp.float32),
            pltpu.VMEM((total, hd), jnp.float32),
        ],
        compiler_params=pltpu.CompilerParams(
            dimension_semantics=("arbitrary",), vmem_limit_bytes=60 << 20),
        cost_estimate=pl.CostEstimate(
            flops=12 * area * hd, bytes_accessed=16 << 20, transcendentals=area),
        name="window_attention",
    )(skip, queries, out_grad, *shards)


moment_decay = 0.8


def shifted(x, axis, by, first=0):
    length = lax.axis_size(axis)
    pairs = [(i, i + by) for i in range(first, length) if 0 <= i + by < length]
    return lax.ppermute(x, axis, pairs)


def after(value, *others):
    return lax.optimization_barrier((value,) + others)[0]


def row_split_refresh(grad_term_sum, moment, left_old, left_new, right_old, right_new):
    turn_share = lax.psum_scatter(
        jnp.einsum("brk,brj->kbj", right_old, right_new, preferred_element_type=jnp.float32),
        "seq", scatter_dimension=0, tiled=True)
    right_turn = jnp.transpose(turn_share, (1, 0, 2)).astype(jnp.bfloat16)
    turned = jnp.einsum(
        "brk,bkj->brj", moment, lax.all_gather(right_turn, "seq", axis=1, tiled=True),
        preferred_element_type=jnp.float32).astype(jnp.bfloat16)
    carried = jnp.einsum(
        "brk,bkj->brj", left_old, lax.all_gather(turned, "seq", axis=1, tiled=True),
        preferred_element_type=jnp.float32)
    grad_term = jnp.einsum(
        "brk,bkj->brj", grad_term_sum, lax.all_gather(right_new, "seq", axis=1, tiled=True),
        preferred_element_type=jnp.float32)
    inner = (moment_decay * carried + (1.0 - moment_decay) * grad_term).astype(jnp.bfloat16)
    new_share = lax.psum_scatter(
        jnp.einsum("brk,brj->kbj", left_new, inner, preferred_element_type=jnp.float32),
        "seq", scatter_dimension=0, tiled=True)
    return jnp.transpose(new_share, (1, 0, 2))


def bmm(spec, a, b):
    return jnp.einsum(spec, a, b, preferred_element_type=jnp.float32)


def project(columns, layer_input):
    return bmm("tj,tk->jk", columns, layer_input).astype(jnp.bfloat16)


def swap_sum(term, n, width):
    index = lax.axis_index("seq")
    if n & (n - 1):
        parts = jnp.stack([term[:, i * width:(i + 1) * width] for i in range(n)])
        return jnp.sum(lax.all_to_all(parts, "seq", 0, 0).astype(jnp.float32), axis=0)
    pieces = [lax.dynamic_slice_in_dim(term, 0, width, 1)] if n == 1 else None
    step = 1
    while step < n:
        mine = (index // step) % 2
        if pieces is None:
            starts = range(n // 2)
            keep = [lax.dynamic_slice_in_dim(term, (2 * i + mine) * width, width, 1) for i in starts]
            send = [lax.dynamic_slice_in_dim(term, (2 * i + 1 - mine) * width, width, 1) for i in starts]
            keep, send = jnp.stack(keep), jnp.stack(send)
        else:
            pairs = pieces.reshape((pieces.shape[0] // 2, 2) + pieces.shape[1:])
            keep = lax.dynamic_index_in_dim(pairs, mine, 1, False)
            send = lax.dynamic_index_in_dim(pairs, 1 - mine, 1, False).astype(jnp.bfloat16)
        got = lax.ppermute(send, "seq", [(i, i ^ step) for i in range(n)])
        pieces = keep.astype(jnp.float32) + got.astype(jnp.float32)
        step *= 2
    return pieces[0].astype(jnp.float32)


def per_device(
    queries, keys, values, out_grad, layer_input, moment, left_old, left_new, right_old, right_new
):
    n = lax.axis_size("seq")
    reach = n // 2
    seq_index = lax.axis_index("seq")
    rows = queries.shape[0]
    hd = HEAD_DIM
    kv_count = keys.shape[1] // hd
    group = queries.shape[1] // keys.shape[1]
    blocks, share_rows, order = moment.shape
    row_blocks = layer_input.shape[1] // order
    whole_blocks = row_blocks % n == 0 and (group + 2) * hd == order
    per_owner = row_blocks // n

    pairs = [
        jnp.concatenate([keys[:, k * hd:(k + 1) * hd], values[:, k * hd:(k + 1) * hd]], axis=1)
        for k in range(kv_count)
    ]
    skip = jnp.reshape(reach - seq_index, (1,)).astype(jnp.int32)

    windows = []
    gate = None
    for k in range(kv_count):
        held = pairs[k] if gate is None else after(pairs[k], gate)
        shards = [pairs[k]]
        if k == 0:
            for hop in range(reach):
                held = shifted(held, "seq", 1, hop)
                shards.insert(0, held)
            gate = held
        else:
            for d in range(1, reach + 1):
                shards.insert(0, shifted(held, "seq", d))
        windows.append(shards)

    if whole_blocks:
        cut = [
            x.reshape(kv_count, n, per_owner, share_rows, order)
            for x in (moment, left_old, left_new, right_old, right_new)
        ]

        def message(owner):
            return jnp.stack([
                lax.dynamic_slice_in_dim(x, owner, 1, 1)[:, 0] for x in cut])

        whole = jnp.zeros((5, kv_count, per_owner, n, share_rows, order), jnp.bfloat16)
        whole = lax.dynamic_update_slice_in_dim(
            whole, message(seq_index)[:, :, :, None], seq_index, 3)
        leftward = []
        for d in range(1, n):
            packed = message((seq_index + n - d) % n)
            if d > 1:
                packed = after(packed, leftward[0])
            leftward.append(shifted(packed, "seq", -d))
        rightward = []
    outs, query_grads, key_grads, value_grads, joined = [], [], [], [], []
    parts_sent = []
    for k in range(kv_count):
        last = k == kv_count - 1
        gate = skip
        if whole_blocks and k < 2:
            gate = after(skip, *(leftward[1:] if k else leftward[:1]))
        head_out, head_dq, *grads = attention(queries, out_grad, gate, windows[k], k, group)
        far, own = grads[:reach], grads[reach]
        outs.append(head_out)
        query_grads.append(head_dq)
        if whole_blocks and k == 0:
            for d in range(1, n):
                packed = after(message((seq_index + d) % n), head_out)
                rightward.append(shifted(packed, "seq", d))
        if not last:
            for d in range(1, reach + 1):
                own = own + shifted(far[reach - d], "seq", -d).astype(jnp.float32)
        else:
            if whole_blocks:
                early = jnp.concatenate(joined + [head_dq], axis=1)
                early_term = swap_sum(project(early, layer_input), n, per_owner * order)
            carry = far[0]
            for d in range(reach, 0, -1):
                carry = shifted(carry, "seq", -1, d)
                if whole_blocks and d == reach:
                    whole = after(whole, carry)
                if d > 1:
                    carry = (carry.astype(jnp.float32) + far[reach - d + 1].astype(jnp.float32)).astype(jnp.bfloat16)
            if whole_blocks:
                for d in range(1, n):
                    source = (seq_index + d) % n
                    piece = jnp.where(seq_index + d < n, leftward[d - 1], rightward[n - d - 1])
                    whole = lax.dynamic_update_slice_in_dim(whole, piece[:, :, :, None], source, 3)
                m_own, lo_own, ln_own, ro_own, rn_own = whole.reshape(
                    5, kv_count, per_owner, order, order)
                right_turn = bmm("cbrk,cbrj->cbkj", ro_own, rn_own).astype(jnp.bfloat16)
                turned = bmm("cbrk,cbkj->cbrj", m_own, right_turn).astype(jnp.bfloat16)
                carried = moment_decay * bmm("cbrk,cbkj->cbrj", lo_own, turned)
                carry = after(carry, carried)
            own = own + carry.astype(jnp.float32)
        kv_grad = own.astype(jnp.bfloat16)
        key_grads.append(kv_grad[:, :hd])
        value_grads.append(kv_grad[:, hd:])
        joined.append(jnp.concatenate([head_dq, kv_grad], axis=1))
    if whole_blocks:
        late_term = swap_sum(project(kv_grad, layer_input), n, per_owner * order)
        grads = jnp.concatenate([early_term, late_term], axis=0).astype(jnp.bfloat16)
        news = []
        for k in range(kv_count):
            grad = grads[k * order:(k + 1) * order].reshape(order, per_owner, order)
            inner = carried[k] + (1.0 - moment_decay) * bmm("jbr,bjk->brk", grad, rn_own[k])
            new = bmm("brk,brj->bkj", ln_own[k], inner.astype(jnp.bfloat16)).astype(jnp.bfloat16)
            new = jnp.transpose(new.reshape(per_owner, n, share_rows, order), (1, 0, 2, 3))
            new = lax.all_to_all(new, "seq", 0, 0)
            news.append(new.reshape(row_blocks, share_rows, order).astype(jnp.float32))
    if whole_blocks:
        new_moment = jnp.concatenate(news, axis=0)
    else:
        joined = jnp.concatenate(joined, axis=1)
        term = bmm(
            "trk,tcj->kcrj",
            layer_input.reshape(rows, row_blocks, order),
            joined.reshape(rows, joined.shape[1] // order, order))
        share = lax.psum_scatter(
            term.reshape(order, blocks, order), "seq", scatter_dimension=0, tiled=True)
        new_moment = row_split_refresh(
            jnp.transpose(share, (1, 0, 2)).astype(jnp.bfloat16),
            moment, left_old, left_new, right_old, right_new)
    join = lambda parts: parts[0] if len(parts) == 1 else jnp.concatenate(parts, axis=1)
    return (join(outs), join(query_grads), join(key_grads), join(value_grads), new_moment)


def solution(mesh):
    both = P(("groups", "seq"), "grid")
    block = P(("groups", "grid"), "seq", None)
    return jax.shard_map(
        per_device,
        mesh=mesh,
        in_specs=(both, both, both, both, P(("groups", "seq"), None)) + (block,) * 5,
        out_specs=(both, both, both, both, block),
        check_vma=False,
    )
```

```python
import functools

import jax
import jax.numpy as jnp
from jax import lax
from jax.experimental import pallas as pl
from jax.experimental.pallas import tpu as pltpu
from jax.sharding import PartitionSpec as P

HEAD_DIM = 128
NEG = -1e30
LOG2E = 1.4426950408889634
NT = (((1,), (1,)), ((), ()))
NN = (((1,), (0,)), ((), ()))


def mm(a, b, dims):
    return lax.dot_general(a, b, dims, preferred_element_type=jnp.float32)


def attn_body(reach, tile, group, skip_ref, q_ref, g_ref, *rest):
    kv_refs = rest[: reach + 1]
    o_ref, dq_ref = rest[reach + 1: reach + 3]
    far_refs = rest[reach + 3: 2 * reach + 3]
    own_ref, kb, vb, kt, vt, s_buf, e_buf, dkt, dvt = rest[2 * reach + 3:]
    hd = HEAD_DIM
    t = pl.program_id(0)
    rows = kv_refs[0].shape[0]
    win = reach * rows
    cols = group * tile
    scale = hd ** -0.5

    @pl.when(t == 0)
    def _():
        first = lax.broadcasted_iota(jnp.int32, (rows, hd), 1) == 0
        for s, ref in enumerate(kv_refs):
            here = pl.ds(s * rows, rows)
            k = ref[:, :hd]
            v = ref[:, hd:]
            kb[here, :hd] = k
            hide = jnp.where(s < skip_ref[0], NEG, 0.0)
            kb[here, hd:] = jnp.where(first, hide, 0.0).astype(jnp.bfloat16)
            vb[here, :] = v
            kt[:, here] = k.T
            vt[:hd, here] = v.T
        vt[hd:, :] = jnp.ones((16, win + rows), jnp.bfloat16)
        dkt[...] = jnp.zeros_like(dkt)
        dvt[...] = jnp.zeros_like(dvt)

    q = jnp.concatenate([q_ref[:, h * hd:(h + 1) * hd] for h in range(group)], axis=0)
    g = jnp.concatenate([g_ref[:, h * hd:(h + 1) * hd] for h in range(group)], axis=0)
    lane = lax.broadcasted_iota(jnp.int32, (cols, hd), 1)
    qa = jnp.concatenate([q, jnp.where(lane == 0, 1.0, 0.0).astype(jnp.bfloat16)], axis=1)
    base = t * tile
    n_full = win - tile

    ki = lax.broadcasted_iota(jnp.int32, (tile, cols), 0)
    qi = lax.broadcasted_iota(jnp.int32, (tile, cols), 1) % tile

    def scores(off, size, keep=None):
        at = pl.ds(pl.multiple_of(base + off, tile), size)
        s = mm(kb[at, :], qa, NT)
        if keep is not None:
            s = jnp.where(keep, s, NEG)
        s_buf[pl.ds(off, size), :] = s
        return jnp.max(s.reshape(size // 8, 8, cols), axis=0)

    m8 = jnp.maximum(scores(0, tile, ki > qi), scores(win, tile, ki <= qi))
    m8 = jnp.maximum(m8, scores(tile, n_full))
    m = jnp.max(m8, axis=0, keepdims=True)
    mc = m * (scale * LOG2E)

    def weigh(off, size):
        at = pl.ds(pl.multiple_of(base + off, tile), size)
        e = jnp.exp2(s_buf[pl.ds(off, size), :] * (scale * LOG2E) - mc).astype(jnp.bfloat16)
        e_buf[pl.ds(off, size), :] = e
        return mm(vt[:, at], e, NN)

    ot = weigh(0, win + tile)
    rl = 1.0 / ot[hd:hd + 1, :]
    on = (ot[:hd, :] * rl).astype(jnp.bfloat16)
    on32 = on.astype(jnp.float32)
    gt = g.astype(jnp.float32).T
    qt = q.astype(jnp.float32).T
    dd = jnp.sum(gt * on32, axis=0, keepdims=True)
    for h in range(group):
        o_ref[:, h * hd:(h + 1) * hd] = on32[:, h * tile:(h + 1) * tile].T.astype(jnp.bfloat16)
    gl = (gt * rl).T.astype(jnp.bfloat16)
    rs = rl * scale
    qr = (qt * rs).T.astype(jnp.bfloat16)

    def back(off, size):
        at = pl.ds(pl.multiple_of(base + off, tile), size)
        e = e_buf[pl.ds(off, size), :]
        dp = mm(vb[at, :], g, NT) - dd
        ds = (e.astype(jnp.float32) * dp).astype(jnp.bfloat16)
        dvt[at, :] += mm(e, gl, NN)
        dkt[at, :] += mm(ds, qr, NN)
        return mm(kt[:, at], ds, NN)

    dqt = back(0, win + tile)
    dqt = dqt * rs
    for h in range(group):
        dq_ref[:, h * hd:(h + 1) * hd] = dqt[:, h * tile:(h + 1) * tile].T.astype(jnp.bfloat16)

    @pl.when(t == pl.num_programs(0) - 1)
    def _():
        for s in range(reach + 1):
            here = pl.ds(s * rows, rows)
            dk = dkt[here, :]
            dv = dvt[here, :]
            if s < reach:
                far_refs[s][:, :hd] = dk.astype(jnp.bfloat16)
                far_refs[s][:, hd:] = dv.astype(jnp.bfloat16)
            else:
                own_ref[:, :hd] = dk
                own_ref[:, hd:] = dv


def attention(queries, out_grad, skip, shards, slot, group, tile=256):
    hd = HEAD_DIM
    rows = queries.shape[0]
    reach = len(shards) - 1
    win = reach * rows
    total = win + rows
    cols = group * tile
    whole = lambda shape: pl.BlockSpec(shape, lambda t: (0, 0), pipeline_mode=pl.Buffered(1))
    part = pl.BlockSpec((tile, group * hd), lambda t: (t, slot))
    outp = pl.BlockSpec((tile, group * hd), lambda t: (t, 0))
    area = win * rows * group
    return pl.pallas_call(
        functools.partial(attn_body, reach, tile, group),
        out_shape=(
            jax.ShapeDtypeStruct((rows, group * hd), jnp.bfloat16),
            jax.ShapeDtypeStruct((rows, group * hd), jnp.bfloat16),
        ) + (jax.ShapeDtypeStruct((rows, 2 * hd), jnp.bfloat16),) * reach + (
            jax.ShapeDtypeStruct((rows, 2 * hd), jnp.float32),
        ),
        grid=(rows // tile,),
        in_specs=[pl.BlockSpec(memory_space=pltpu.SMEM), part, part] + [whole((rows, 2 * hd))] * (reach + 1),
        out_specs=(outp, outp) + (whole((rows, 2 * hd)),) * (reach + 1),
        scratch_shapes=[
            pltpu.VMEM((total, 2 * hd), jnp.bfloat16),
            pltpu.VMEM((total, hd), jnp.bfloat16),
            pltpu.VMEM((hd, total), jnp.bfloat16),
            pltpu.VMEM((hd + 16, total), jnp.bfloat16),
            pltpu.VMEM((win + tile, cols), jnp.float32),
            pltpu.VMEM((win + tile, cols), jnp.bfloat16),
            pltpu.VMEM((total, hd), jnp.float32),
            pltpu.VMEM((total, hd), jnp.float32),
        ],
        compiler_params=pltpu.CompilerParams(
            dimension_semantics=("arbitrary",), vmem_limit_bytes=60 << 20),
        cost_estimate=pl.CostEstimate(
            flops=12 * area * hd, bytes_accessed=16 << 20, transcendentals=area),
        name="window_attention",
    )(skip, queries, out_grad, *shards)


moment_decay = 0.8


def shifted(x, axis, by, first=0):
    length = lax.axis_size(axis)
    pairs = [(i, i + by) for i in range(first, length) if 0 <= i + by < length]
    return lax.ppermute(x, axis, pairs)


def after(value, *others):
    return lax.optimization_barrier((value,) + others)[0]


def row_split_refresh(grad_term_sum, moment, left_old, left_new, right_old, right_new):
    turn_share = lax.psum_scatter(
        jnp.einsum("brk,brj->kbj", right_old, right_new, preferred_element_type=jnp.float32),
        "seq", scatter_dimension=0, tiled=True)
    right_turn = jnp.transpose(turn_share, (1, 0, 2)).astype(jnp.bfloat16)
    turned = jnp.einsum(
        "brk,bkj->brj", moment, lax.all_gather(right_turn, "seq", axis=1, tiled=True),
        preferred_element_type=jnp.float32).astype(jnp.bfloat16)
    carried = jnp.einsum(
        "brk,bkj->brj", left_old, lax.all_gather(turned, "seq", axis=1, tiled=True),
        preferred_element_type=jnp.float32)
    grad_term = jnp.einsum(
        "brk,bkj->brj", grad_term_sum, lax.all_gather(right_new, "seq", axis=1, tiled=True),
        preferred_element_type=jnp.float32)
    inner = (moment_decay * carried + (1.0 - moment_decay) * grad_term).astype(jnp.bfloat16)
    new_share = lax.psum_scatter(
        jnp.einsum("brk,brj->kbj", left_new, inner, preferred_element_type=jnp.float32),
        "seq", scatter_dimension=0, tiled=True)
    return jnp.transpose(new_share, (1, 0, 2))


def bmm(spec, a, b):
    return jnp.einsum(spec, a, b, preferred_element_type=jnp.float32)


def project(columns, layer_input):
    return bmm("tj,tk->jk", columns, layer_input).astype(jnp.bfloat16)


def swap_sum(term, n, width, sent=None):
    index = lax.axis_index("seq")
    if n & (n - 1):
        parts = jnp.stack([term[:, i * width:(i + 1) * width] for i in range(n)])
        return jnp.sum(lax.all_to_all(parts, "seq", 0, 0).astype(jnp.float32), axis=0)
    pieces = [lax.dynamic_slice_in_dim(term, 0, width, 1)] if n == 1 else None
    step = 1
    while step < n:
        mine = (index // step) % 2
        if pieces is None:
            starts = range(n // 2)
            keep = [lax.dynamic_slice_in_dim(term, (2 * i + mine) * width, width, 1) for i in starts]
            send = [lax.dynamic_slice_in_dim(term, (2 * i + 1 - mine) * width, width, 1) for i in starts]
            keep, send = jnp.stack(keep), jnp.stack(send)
        else:
            pairs = pieces.reshape((pieces.shape[0] // 2, 2) + pieces.shape[1:])
            keep = lax.dynamic_index_in_dim(pairs, mine, 1, False)
            send = lax.dynamic_index_in_dim(pairs, 1 - mine, 1, False).astype(jnp.bfloat16)
        if sent is not None:
            sent.append(send)
        got = lax.ppermute(send, "seq", [(i, i ^ step) for i in range(n)])
        pieces = keep.astype(jnp.float32) + got.astype(jnp.float32)
        step *= 2
    return pieces[0].astype(jnp.float32)


def per_device(
    queries, keys, values, out_grad, layer_input, moment, left_old, left_new, right_old, right_new
):
    n = lax.axis_size("seq")
    reach = n // 2
    seq_index = lax.axis_index("seq")
    rows = queries.shape[0]
    hd = HEAD_DIM
    kv_count = keys.shape[1] // hd
    group = queries.shape[1] // keys.shape[1]
    blocks, share_rows, order = moment.shape
    row_blocks = layer_input.shape[1] // order
    whole_blocks = row_blocks % n == 0 and (group + 2) * hd == order
    per_owner = row_blocks // n

    pairs = [
        jnp.concatenate([keys[:, k * hd:(k + 1) * hd], values[:, k * hd:(k + 1) * hd]], axis=1)
        for k in range(kv_count)
    ]
    skip = jnp.reshape(reach - seq_index, (1,)).astype(jnp.int32)

    windows = []
    gate = None
    for k in range(kv_count):
        held = pairs[k] if gate is None else after(pairs[k], gate)
        shards = [pairs[k]]
        if k == 0:
            for hop in range(reach):
                held = shifted(held, "seq", 1, hop)
                shards.insert(0, held)
            gate = held
        else:
            for d in range(1, reach + 1):
                shards.insert(0, shifted(held, "seq", d))
        windows.append(shards)

    if whole_blocks:
        cut = [
            x.reshape(kv_count, n, per_owner, share_rows, order)
            for x in (moment, left_old, left_new, right_old, right_new)
        ]

        def message(owner):
            return jnp.stack([
                lax.dynamic_slice_in_dim(x, owner, 1, 1)[:, 0] for x in cut])

        whole = jnp.zeros((5, kv_count, per_owner, n, share_rows, order), jnp.bfloat16)
        whole = lax.dynamic_update_slice_in_dim(
            whole, message(seq_index)[:, :, :, None], seq_index, 3)
        leftward = []
        for d in range(1, n):
            packed = message((seq_index + n - d) % n)
            if d > 1:
                packed = after(packed, leftward[0])
            leftward.append(shifted(packed, "seq", -d))
        rightward = []
    outs, query_grads, key_grads, value_grads, joined = [], [], [], [], []
    parts_sent = []
    for k in range(kv_count):
        last = k == kv_count - 1
        gate = skip
        if whole_blocks and k < 2:
            gate = after(skip, *(leftward[1:] if k else leftward[:1]))
        head_out, head_dq, *grads = attention(queries, out_grad, gate, windows[k], k, group)
        far, own = grads[:reach], grads[reach]
        outs.append(head_out)
        query_grads.append(head_dq)
        if whole_blocks and k == 0:
            for d in range(1, n):
                packed = after(message((seq_index + d) % n), head_out)
                rightward.append(shifted(packed, "seq", d))
        if whole_blocks and last:
            back = [shifted(far[reach - d], "seq", -d) for d in range(1, reach + 1)]
            early = jnp.concatenate(joined + [head_dq], axis=1)
            sent = []
            early_term = swap_sum(project(early, layer_input), n, per_owner * order, sent)
            for d in range(1, n):
                source = (seq_index + d) % n
                piece = jnp.where(seq_index + d < n, leftward[d - 1], rightward[n - d - 1])
                whole = lax.dynamic_update_slice_in_dim(whole, piece[:, :, :, None], source, 3)
            m_own, lo_own, ln_own, ro_own, rn_own = whole.reshape(
                5, kv_count, per_owner, order, order)
            right_turn = bmm("cbrk,cbrj->cbkj", ro_own, rn_own).astype(jnp.bfloat16)
            turned = bmm("cbrk,cbkj->cbrj", m_own, right_turn).astype(jnp.bfloat16)
            carried = moment_decay * bmm("cbrk,cbkj->cbrj", lo_own, turned)
            back[0] = after(back[0], carried, *sent)
        elif last and kv_count == 1:
            carry = far[0]
            for d in range(reach, 0, -1):
                carry = shifted(carry, "seq", -1, d)
                if d > 1:
                    carry = (carry.astype(jnp.float32) + far[reach - d + 1].astype(jnp.float32)).astype(jnp.bfloat16)
            back = [carry]
        else:
            back = [shifted(far[reach - d], "seq", -d) for d in range(1, reach + 1)]
        for piece in back:
            own = own + piece.astype(jnp.float32)
        kv_grad = own.astype(jnp.bfloat16)
        key_grads.append(kv_grad[:, :hd])
        value_grads.append(kv_grad[:, hd:])
        joined.append(jnp.concatenate([head_dq, kv_grad], axis=1))
    if whole_blocks:
        late_term = swap_sum(project(kv_grad, layer_input), n, per_owner * order)
        news = []
        ready = None
        for k in range(kv_count):
            grad = early_term[k * order:(k + 1) * order]
            if k == kv_count - 1:
                late = late_term if ready is None else after(late_term, ready)
                grad = jnp.concatenate([grad, late], axis=0)
            grad = grad.astype(jnp.bfloat16).reshape(order, per_owner, order)
            inner = carried[k] + (1.0 - moment_decay) * bmm("jbr,bjk->brk", grad, rn_own[k])
            new = bmm("brk,brj->bkj", ln_own[k], inner.astype(jnp.bfloat16)).astype(jnp.bfloat16)
            new = jnp.transpose(new.reshape(per_owner, n, share_rows, order), (1, 0, 2, 3))
            ready = new
            new = lax.all_to_all(new, "seq", 0, 0)
            news.append(new.reshape(row_blocks, share_rows, order).astype(jnp.float32))
    if whole_blocks:
        new_moment = jnp.concatenate(news, axis=0)
    else:
        joined = jnp.concatenate(joined, axis=1)
        term = bmm(
            "trk,tcj->kcrj",
            layer_input.reshape(rows, row_blocks, order),
            joined.reshape(rows, joined.shape[1] // order, order))
        share = lax.psum_scatter(
            term.reshape(order, blocks, order), "seq", scatter_dimension=0, tiled=True)
        new_moment = row_split_refresh(
            jnp.transpose(share, (1, 0, 2)).astype(jnp.bfloat16),
            moment, left_old, left_new, right_old, right_new)
    join = lambda parts: parts[0] if len(parts) == 1 else jnp.concatenate(parts, axis=1)
    return (join(outs), join(query_grads), join(key_grads), join(value_grads), new_moment)


def solution(mesh):
    both = P(("groups", "seq"), "grid")
    block = P(("groups", "grid"), "seq", None)
    return jax.shard_map(
        per_device,
        mesh=mesh,
        in_specs=(both, both, both, both, P(("groups", "seq"), None)) + (block,) * 5,
        out_specs=(both, both, both, both, block),
        check_vma=False,
    )
```

```python
import functools

import jax
import jax.numpy as jnp
from jax import lax
from jax.experimental import pallas as pl
from jax.experimental.pallas import tpu as pltpu
from jax.sharding import PartitionSpec as P

HEAD_DIM = 128
NEG = -1e30
LOG2E = 1.4426950408889634
NT = (((1,), (1,)), ((), ()))
NN = (((1,), (0,)), ((), ()))


def mm(a, b, dims):
    return lax.dot_general(a, b, dims, preferred_element_type=jnp.float32)


def attn_body(reach, tile, group, skip_ref, q_ref, g_ref, *rest):
    kv_refs = rest[: reach + 1]
    o_ref, dq_ref = rest[reach + 1: reach + 3]
    far_refs = rest[reach + 3: 2 * reach + 3]
    own_ref, kb, vb, kt, vt, s_buf, e_buf, dkt, dvt = rest[2 * reach + 3:]
    hd = HEAD_DIM
    t = pl.program_id(0)
    rows = kv_refs[0].shape[0]
    win = reach * rows
    cols = group * tile
    scale = hd ** -0.5

    @pl.when(t == 0)
    def _():
        first = lax.broadcasted_iota(jnp.int32, (rows, hd), 1) == 0
        for s, ref in enumerate(kv_refs):
            here = pl.ds(s * rows, rows)
            k = ref[:, :hd]
            v = ref[:, hd:]
            kb[here, :hd] = k
            hide = jnp.where(s < skip_ref[0], NEG, 0.0)
            kb[here, hd:] = jnp.where(first, hide, 0.0).astype(jnp.bfloat16)
            vb[here, :] = v
            kt[:, here] = k.T
            vt[:hd, here] = v.T
        vt[hd:, :] = jnp.ones((16, win + rows), jnp.bfloat16)
        dkt[...] = jnp.zeros_like(dkt)
        dvt[...] = jnp.zeros_like(dvt)

    q = jnp.concatenate([q_ref[:, h * hd:(h + 1) * hd] for h in range(group)], axis=0)
    g = jnp.concatenate([g_ref[:, h * hd:(h + 1) * hd] for h in range(group)], axis=0)
    lane = lax.broadcasted_iota(jnp.int32, (cols, hd), 1)
    qa = jnp.concatenate([q, jnp.where(lane == 0, 1.0, 0.0).astype(jnp.bfloat16)], axis=1)
    base = t * tile
    n_full = win - tile

    ki = lax.broadcasted_iota(jnp.int32, (tile, cols), 0)
    qi = lax.broadcasted_iota(jnp.int32, (tile, cols), 1) % tile

    def scores(off, size, keep=None):
        at = pl.ds(pl.multiple_of(base + off, tile), size)
        s = mm(kb[at, :], qa, NT)
        if keep is not None:
            s = jnp.where(keep, s, NEG)
        s_buf[pl.ds(off, size), :] = s
        return jnp.max(s.reshape(size // 8, 8, cols), axis=0)

    m8 = jnp.maximum(scores(0, tile, ki > qi), scores(win, tile, ki <= qi))
    m8 = jnp.maximum(m8, scores(tile, n_full))
    m = jnp.max(m8, axis=0, keepdims=True)
    mc = m * (scale * LOG2E)

    def weigh(off, size):
        at = pl.ds(pl.multiple_of(base + off, tile), size)
        e = jnp.exp2(s_buf[pl.ds(off, size), :] * (scale * LOG2E) - mc).astype(jnp.bfloat16)
        e_buf[pl.ds(off, size), :] = e
        return mm(vt[:, at], e, NN)

    ot = weigh(0, win + tile)
    rl = 1.0 / ot[hd:hd + 1, :]
    on = (ot[:hd, :] * rl).astype(jnp.bfloat16)
    on32 = on.astype(jnp.float32)
    gt = g.astype(jnp.float32).T
    qt = q.astype(jnp.float32).T
    dd = jnp.sum(gt * on32, axis=0, keepdims=True)
    for h in range(group):
        o_ref[:, h * hd:(h + 1) * hd] = on32[:, h * tile:(h + 1) * tile].T.astype(jnp.bfloat16)
    gl = (gt * rl).T.astype(jnp.bfloat16)
    rs = rl * scale
    qr = (qt * rs).T.astype(jnp.bfloat16)

    def back(off, size):
        at = pl.ds(pl.multiple_of(base + off, tile), size)
        e = e_buf[pl.ds(off, size), :]
        dp = mm(vb[at, :], g, NT) - dd
        ds = (e.astype(jnp.float32) * dp).astype(jnp.bfloat16)
        dvt[at, :] += mm(e, gl, NN)
        dkt[at, :] += mm(ds, qr, NN)
        return mm(kt[:, at], ds, NN)

    dqt = back(0, win + tile)
    dqt = dqt * rs
    for h in range(group):
        dq_ref[:, h * hd:(h + 1) * hd] = dqt[:, h * tile:(h + 1) * tile].T.astype(jnp.bfloat16)

    @pl.when(t == pl.num_programs(0) - 1)
    def _():
        for s in range(reach + 1):
            here = pl.ds(s * rows, rows)
            dk = dkt[here, :]
            dv = dvt[here, :]
            if s < reach:
                far_refs[s][:, :hd] = dk.astype(jnp.bfloat16)
                far_refs[s][:, hd:] = dv.astype(jnp.bfloat16)
            else:
                own_ref[:, :hd] = dk
                own_ref[:, hd:] = dv


def attention(queries, out_grad, skip, shards, slot, group, tile=256):
    hd = HEAD_DIM
    rows = queries.shape[0]
    reach = len(shards) - 1
    win = reach * rows
    total = win + rows
    cols = group * tile
    whole = lambda shape: pl.BlockSpec(shape, lambda t: (0, 0), pipeline_mode=pl.Buffered(1))
    part = pl.BlockSpec((tile, group * hd), lambda t: (t, slot))
    outp = pl.BlockSpec((tile, group * hd), lambda t: (t, 0))
    area = win * rows * group
    return pl.pallas_call(
        functools.partial(attn_body, reach, tile, group),
        out_shape=(
            jax.ShapeDtypeStruct((rows, group * hd), jnp.bfloat16),
            jax.ShapeDtypeStruct((rows, group * hd), jnp.bfloat16),
        ) + (jax.ShapeDtypeStruct((rows, 2 * hd), jnp.bfloat16),) * reach + (
            jax.ShapeDtypeStruct((rows, 2 * hd), jnp.float32),
        ),
        grid=(rows // tile,),
        in_specs=[pl.BlockSpec(memory_space=pltpu.SMEM), part, part] + [whole((rows, 2 * hd))] * (reach + 1),
        out_specs=(outp, outp) + (whole((rows, 2 * hd)),) * (reach + 1),
        scratch_shapes=[
            pltpu.VMEM((total, 2 * hd), jnp.bfloat16),
            pltpu.VMEM((total, hd), jnp.bfloat16),
            pltpu.VMEM((hd, total), jnp.bfloat16),
            pltpu.VMEM((hd + 16, total), jnp.bfloat16),
            pltpu.VMEM((win + tile, cols), jnp.float32),
            pltpu.VMEM((win + tile, cols), jnp.bfloat16),
            pltpu.VMEM((total, hd), jnp.float32),
            pltpu.VMEM((total, hd), jnp.float32),
        ],
        compiler_params=pltpu.CompilerParams(
            dimension_semantics=("arbitrary",), vmem_limit_bytes=60 << 20),
        cost_estimate=pl.CostEstimate(
            flops=12 * area * hd, bytes_accessed=16 << 20, transcendentals=area),
        name="window_attention",
    )(skip, queries, out_grad, *shards)


moment_decay = 0.8


def shifted(x, axis, by, first=0):
    length = lax.axis_size(axis)
    pairs = [(i, i + by) for i in range(first, length) if 0 <= i + by < length]
    return lax.ppermute(x, axis, pairs)


def after(value, *others):
    return lax.optimization_barrier((value,) + others)[0]


def row_split_refresh(grad_term_sum, moment, left_old, left_new, right_old, right_new):
    turn_share = lax.psum_scatter(
        jnp.einsum("brk,brj->kbj", right_old, right_new, preferred_element_type=jnp.float32),
        "seq", scatter_dimension=0, tiled=True)
    right_turn = jnp.transpose(turn_share, (1, 0, 2)).astype(jnp.bfloat16)
    turned = jnp.einsum(
        "brk,bkj->brj", moment, lax.all_gather(right_turn, "seq", axis=1, tiled=True),
        preferred_element_type=jnp.float32).astype(jnp.bfloat16)
    carried = jnp.einsum(
        "brk,bkj->brj", left_old, lax.all_gather(turned, "seq", axis=1, tiled=True),
        preferred_element_type=jnp.float32)
    grad_term = jnp.einsum(
        "brk,bkj->brj", grad_term_sum, lax.all_gather(right_new, "seq", axis=1, tiled=True),
        preferred_element_type=jnp.float32)
    inner = (moment_decay * carried + (1.0 - moment_decay) * grad_term).astype(jnp.bfloat16)
    new_share = lax.psum_scatter(
        jnp.einsum("brk,brj->kbj", left_new, inner, preferred_element_type=jnp.float32),
        "seq", scatter_dimension=0, tiled=True)
    return jnp.transpose(new_share, (1, 0, 2))


def bmm(spec, a, b):
    return jnp.einsum(spec, a, b, preferred_element_type=jnp.float32)


def pack_body(owner_ref, *refs):
    del owner_ref
    for i, ref in enumerate(refs[:-1]):
        refs[-1][i] = ref[:, 0]


def pack(owner, arrays):
    heads, _, blocks, rows, order = arrays[0].shape
    shape = (len(arrays), heads, blocks, rows, order)
    return pl.pallas_call(
        pack_body,
        out_shape=jax.ShapeDtypeStruct(shape, arrays[0].dtype),
        grid_spec=pltpu.PrefetchScalarGridSpec(
            num_scalar_prefetch=1,
            grid=(1,),
            in_specs=[pl.BlockSpec(
                (heads, 1, blocks, rows, order), lambda i, who: (0, who[0], 0, 0, 0))] * len(arrays),
            out_specs=pl.BlockSpec(shape, lambda i, who: (0,) * 5),
        ),
        compiler_params=pltpu.CompilerParams(vmem_limit_bytes=32 << 20),
        cost_estimate=pl.CostEstimate(
            flops=1 << 20, bytes_accessed=4 << 20, transcendentals=0),
        name="pack_blocks",
    )(jnp.reshape(owner, (1,)).astype(jnp.int32), *arrays)


def project(columns, layer_input):
    return bmm("tj,tk->jk", columns, layer_input).astype(jnp.bfloat16)


def swap_sum(term, n, width, hold=None):
    index = lax.axis_index("seq")
    if n & (n - 1):
        parts = jnp.stack([term[:, i * width:(i + 1) * width] for i in range(n)])
        return jnp.sum(lax.all_to_all(parts, "seq", 0, 0).astype(jnp.float32), axis=0)
    pieces = [lax.dynamic_slice_in_dim(term, 0, width, 1)] if n == 1 else None
    step = 1
    while step < n:
        mine = (index // step) % 2
        if pieces is None:
            starts = range(n // 2)
            keep = [lax.dynamic_slice_in_dim(term, (2 * i + mine) * width, width, 1) for i in starts]
            send = [lax.dynamic_slice_in_dim(term, (2 * i + 1 - mine) * width, width, 1) for i in starts]
            keep, send = jnp.stack(keep), jnp.stack(send)
        else:
            pairs = pieces.reshape((pieces.shape[0] // 2, 2) + pieces.shape[1:])
            keep = lax.dynamic_index_in_dim(pairs, mine, 1, False)
            send = lax.dynamic_index_in_dim(pairs, 1 - mine, 1, False).astype(jnp.bfloat16)
        if hold is not None and step > 1:
            send = after(send, hold)
        got = lax.ppermute(send, "seq", [(i, i ^ step) for i in range(n)])
        pieces = keep.astype(jnp.float32) + got.astype(jnp.float32)
        step *= 2
    return pieces[0].astype(jnp.float32)


def per_device(
    queries, keys, values, out_grad, layer_input, moment, left_old, left_new, right_old, right_new
):
    n = lax.axis_size("seq")
    reach = n // 2
    seq_index = lax.axis_index("seq")
    rows = queries.shape[0]
    hd = HEAD_DIM
    kv_count = keys.shape[1] // hd
    group = queries.shape[1] // keys.shape[1]
    blocks, share_rows, order = moment.shape
    row_blocks = layer_input.shape[1] // order
    whole_blocks = row_blocks % n == 0 and (group + 2) * hd == order
    per_owner = row_blocks // n

    pairs = [
        jnp.concatenate([keys[:, k * hd:(k + 1) * hd], values[:, k * hd:(k + 1) * hd]], axis=1)
        for k in range(kv_count)
    ]
    skip = jnp.reshape(reach - seq_index, (1,)).astype(jnp.int32)

    windows = []
    shards = [pairs[0]]
    for hop in range(reach):
        shards.insert(0, shifted(shards[0], "seq", 1, hop))
    windows.append(shards)
    gate = shards[0]

    if whole_blocks:
        cut = [
            x.reshape(kv_count, n, per_owner, share_rows, order)
            for x in (moment, left_old, left_new, right_old, right_new)
        ]

        def message(owner):
            return jnp.stack([
                lax.dynamic_slice_in_dim(x, owner, 1, 1)[:, 0] for x in cut])

        whole = jnp.zeros((5, kv_count, per_owner, n, share_rows, order), jnp.bfloat16)
        whole = lax.dynamic_update_slice_in_dim(
            whole, message(seq_index)[:, :, :, None], seq_index, 3)
        leftward = []
        for d in range(1, n):
            owner = (seq_index + n - d) % n
            packed = after(message(owner), leftward[0]) if d > 1 else pack(owner, cut)
            leftward.append(shifted(packed, "seq", -d))
        rightward = []
    if whole_blocks:
        gate = leftward[0]
    for k in range(1, kv_count):
        held = after(pairs[k], gate)
        windows.append([shifted(held, "seq", d) for d in range(reach, 0, -1)] + [pairs[k]])

    outs, query_grads, key_grads, value_grads, joined = [], [], [], [], []
    parts_sent = []
    for k in range(kv_count):
        last = k == kv_count - 1
        gate = skip
        if whole_blocks and k < 2:
            gate = after(skip, *(leftward[1:] if k else leftward[:1]))
        head_out, head_dq, *grads = attention(queries, out_grad, gate, windows[k], k, group)
        far, own = grads[:reach], grads[reach]
        outs.append(head_out)
        query_grads.append(head_dq)
        if whole_blocks and k == 0:
            for d in range(1, n):
                packed = after(message((seq_index + d) % n), head_out)
                rightward.append(shifted(packed, "seq", d))
        if not last:
            for d in range(1, reach + 1):
                own = own + shifted(far[reach - d], "seq", -d).astype(jnp.float32)
        else:
            if whole_blocks:
                early = jnp.concatenate(joined + [head_dq], axis=1)
                early_term = swap_sum(project(early, layer_input), n, per_owner * order)
            carry = far[0]
            for d in range(reach, 0, -1):
                carry = shifted(carry, "seq", -1, d)
                if whole_blocks and d == reach:
                    whole = after(whole, carry)
                if d > 1:
                    carry = (carry.astype(jnp.float32) + far[reach - d + 1].astype(jnp.float32)).astype(jnp.bfloat16)
            if whole_blocks:
                for d in range(1, n):
                    source = (seq_index + d) % n
                    piece = jnp.where(seq_index + d < n, leftward[d - 1], rightward[n - d - 1])
                    whole = lax.dynamic_update_slice_in_dim(whole, piece[:, :, :, None], source, 3)
                m_own, lo_own, ln_own, ro_own, rn_own = whole.reshape(
                    5, kv_count, per_owner, order, order)
                right_turn = bmm("cbrk,cbrj->cbkj", ro_own, rn_own).astype(jnp.bfloat16)
                turned = bmm("cbrk,cbkj->cbrj", m_own, right_turn).astype(jnp.bfloat16)
                carried = moment_decay * bmm("cbrk,cbkj->cbrj", lo_own, turned)
                carry = after(carry, carried)
            own = own + carry.astype(jnp.float32)
        kv_grad = own.astype(jnp.bfloat16)
        key_grads.append(kv_grad[:, :hd])
        value_grads.append(kv_grad[:, hd:])
        joined.append(jnp.concatenate([head_dq, kv_grad], axis=1))
    if whole_blocks:
        news = []
        ready = None
        for k in range(kv_count):
            grad = early_term[k * order:(k + 1) * order]
            if k == kv_count - 1:
                late_term = swap_sum(
                    project(kv_grad, layer_input), n, per_owner * order, ready)
                grad = jnp.concatenate([grad, late_term], axis=0)
            grad = grad.astype(jnp.bfloat16).reshape(order, per_owner, order)
            inner = carried[k] + (1.0 - moment_decay) * bmm("jbr,bjk->brk", grad, rn_own[k])
            new = bmm("brk,brj->bkj", ln_own[k], inner.astype(jnp.bfloat16)).astype(jnp.bfloat16)
            new = jnp.transpose(new.reshape(per_owner, n, share_rows, order), (1, 0, 2, 3))
            ready = new
            new = lax.all_to_all(new, "seq", 0, 0)
            news.append(new.reshape(row_blocks, share_rows, order).astype(jnp.float32))
    if whole_blocks:
        new_moment = jnp.concatenate(news, axis=0)
    else:
        joined = jnp.concatenate(joined, axis=1)
        term = bmm(
            "trk,tcj->kcrj",
            layer_input.reshape(rows, row_blocks, order),
            joined.reshape(rows, joined.shape[1] // order, order))
        share = lax.psum_scatter(
            term.reshape(order, blocks, order), "seq", scatter_dimension=0, tiled=True)
        new_moment = row_split_refresh(
            jnp.transpose(share, (1, 0, 2)).astype(jnp.bfloat16),
            moment, left_old, left_new, right_old, right_new)
    join = lambda parts: parts[0] if len(parts) == 1 else jnp.concatenate(parts, axis=1)
    return (join(outs), join(query_grads), join(key_grads), join(value_grads), new_moment)


def solution(mesh):
    both = P(("groups", "seq"), "grid")
    block = P(("groups", "grid"), "seq", None)
    return jax.shard_map(
        per_device,
        mesh=mesh,
        in_specs=(both, both, both, both, P(("groups", "seq"), None)) + (block,) * 5,
        out_specs=(both, both, both, both, block),
        check_vma=False,
    )
```

```python
import functools

import jax
import jax.numpy as jnp
from jax import lax
from jax.experimental import pallas as pl
from jax.experimental.pallas import tpu as pltpu
from jax.sharding import PartitionSpec as P

HEAD_DIM = 128
NEG = -1e30
LOG2E = 1.4426950408889634
NT = (((1,), (1,)), ((), ()))
NN = (((1,), (0,)), ((), ()))


def mm(a, b, dims):
    return lax.dot_general(a, b, dims, preferred_element_type=jnp.float32)


def attn_body(reach, tile, group, skip_ref, q_ref, g_ref, *rest):
    kv_refs = rest[: reach + 1]
    o_ref, dq_ref = rest[reach + 1: reach + 3]
    far_refs = rest[reach + 3: 2 * reach + 3]
    own_ref, kb, vb, kt, vt, s_buf, e_buf, dkt, dvt = rest[2 * reach + 3:]
    hd = HEAD_DIM
    t = pl.program_id(0)
    rows = kv_refs[0].shape[0]
    win = reach * rows
    cols = group * tile
    scale = hd ** -0.5

    @pl.when(t == 0)
    def _():
        first = lax.broadcasted_iota(jnp.int32, (rows, hd), 1) == 0
        for s, ref in enumerate(kv_refs):
            here = pl.ds(s * rows, rows)
            k = ref[:, :hd]
            v = ref[:, hd:]
            kb[here, :hd] = k
            hide = jnp.where(s < skip_ref[0], NEG, 0.0)
            kb[here, hd:] = jnp.where(first, hide, 0.0).astype(jnp.bfloat16)
            vb[here, :] = v
            kt[:, here] = k.T
            vt[:hd, here] = v.T
        vt[hd:, :] = jnp.ones((16, win + rows), jnp.bfloat16)
        dkt[...] = jnp.zeros_like(dkt)
        dvt[...] = jnp.zeros_like(dvt)

    q = jnp.concatenate([q_ref[:, h * hd:(h + 1) * hd] for h in range(group)], axis=0)
    g = jnp.concatenate([g_ref[:, h * hd:(h + 1) * hd] for h in range(group)], axis=0)
    lane = lax.broadcasted_iota(jnp.int32, (cols, hd), 1)
    qa = jnp.concatenate([q, jnp.where(lane == 0, 1.0, 0.0).astype(jnp.bfloat16)], axis=1)
    base = t * tile
    n_full = win - tile

    ki = lax.broadcasted_iota(jnp.int32, (tile, cols), 0)
    qi = lax.broadcasted_iota(jnp.int32, (tile, cols), 1) % tile

    def scores(off, size, keep=None):
        at = pl.ds(pl.multiple_of(base + off, tile), size)
        s = mm(kb[at, :], qa, NT)
        if keep is not None:
            s = jnp.where(keep, s, NEG)
        s_buf[pl.ds(off, size), :] = s
        return jnp.max(s.reshape(size // 8, 8, cols), axis=0)

    m8 = jnp.maximum(scores(0, tile, ki > qi), scores(win, tile, ki <= qi))
    m8 = jnp.maximum(m8, scores(tile, n_full))
    m = jnp.max(m8, axis=0, keepdims=True)
    mc = m * (scale * LOG2E)

    def weigh(off, size):
        at = pl.ds(pl.multiple_of(base + off, tile), size)
        e = jnp.exp2(s_buf[pl.ds(off, size), :] * (scale * LOG2E) - mc).astype(jnp.bfloat16)
        e_buf[pl.ds(off, size), :] = e
        return mm(vt[:, at], e, NN)

    ot = weigh(0, win + tile)
    rl = 1.0 / ot[hd:hd + 1, :]
    on = (ot[:hd, :] * rl).astype(jnp.bfloat16)
    on32 = on.astype(jnp.float32)
    gt = g.astype(jnp.float32).T
    qt = q.astype(jnp.float32).T
    dd = jnp.sum(gt * on32, axis=0, keepdims=True)
    for h in range(group):
        o_ref[:, h * hd:(h + 1) * hd] = on32[:, h * tile:(h + 1) * tile].T.astype(jnp.bfloat16)
    gl = (gt * rl).T.astype(jnp.bfloat16)
    rs = rl * scale
    qr = (qt * rs).T.astype(jnp.bfloat16)

    def back(off, size):
        at = pl.ds(pl.multiple_of(base + off, tile), size)
        e = e_buf[pl.ds(off, size), :]
        dp = mm(vb[at, :], g, NT) - dd
        ds = (e.astype(jnp.float32) * dp).astype(jnp.bfloat16)
        dvt[at, :] += mm(e, gl, NN)
        dkt[at, :] += mm(ds, qr, NN)
        return mm(kt[:, at], ds, NN)

    dqt = back(0, win + tile)
    dqt = dqt * rs
    for h in range(group):
        dq_ref[:, h * hd:(h + 1) * hd] = dqt[:, h * tile:(h + 1) * tile].T.astype(jnp.bfloat16)

    @pl.when(t == pl.num_programs(0) - 1)
    def _():
        for s in range(reach + 1):
            here = pl.ds(s * rows, rows)
            dk = dkt[here, :]
            dv = dvt[here, :]
            if s < reach:
                far_refs[s][:, :hd] = dk.astype(jnp.bfloat16)
                far_refs[s][:, hd:] = dv.astype(jnp.bfloat16)
            else:
                own_ref[:, :hd] = dk
                own_ref[:, hd:] = dv


def attention(queries, out_grad, skip, shards, slot, group, tile=256):
    hd = HEAD_DIM
    rows = queries.shape[0]
    reach = len(shards) - 1
    win = reach * rows
    total = win + rows
    cols = group * tile
    whole = lambda shape: pl.BlockSpec(shape, lambda t: (0, 0), pipeline_mode=pl.Buffered(1))
    part = pl.BlockSpec((tile, group * hd), lambda t: (t, slot))
    outp = pl.BlockSpec((tile, group * hd), lambda t: (t, 0))
    area = win * rows * group
    return pl.pallas_call(
        functools.partial(attn_body, reach, tile, group),
        out_shape=(
            jax.ShapeDtypeStruct((rows, group * hd), jnp.bfloat16),
            jax.ShapeDtypeStruct((rows, group * hd), jnp.bfloat16),
        ) + (jax.ShapeDtypeStruct((rows, 2 * hd), jnp.bfloat16),) * reach + (
            jax.ShapeDtypeStruct((rows, 2 * hd), jnp.float32),
        ),
        grid=(rows // tile,),
        in_specs=[pl.BlockSpec(memory_space=pltpu.SMEM), part, part] + [whole((rows, 2 * hd))] * (reach + 1),
        out_specs=(outp, outp) + (whole((rows, 2 * hd)),) * (reach + 1),
        scratch_shapes=[
            pltpu.VMEM((total, 2 * hd), jnp.bfloat16),
            pltpu.VMEM((total, hd), jnp.bfloat16),
            pltpu.VMEM((hd, total), jnp.bfloat16),
            pltpu.VMEM((hd + 16, total), jnp.bfloat16),
            pltpu.VMEM((win + tile, cols), jnp.float32),
            pltpu.VMEM((win + tile, cols), jnp.bfloat16),
            pltpu.VMEM((total, hd), jnp.float32),
            pltpu.VMEM((total, hd), jnp.float32),
        ],
        compiler_params=pltpu.CompilerParams(
            dimension_semantics=("arbitrary",), vmem_limit_bytes=60 << 20),
        cost_estimate=pl.CostEstimate(
            flops=12 * area * hd, bytes_accessed=16 << 20, transcendentals=area),
        name="window_attention",
    )(skip, queries, out_grad, *shards)


moment_decay = 0.8


def shifted(x, axis, by, first=0):
    length = lax.axis_size(axis)
    pairs = [(i, i + by) for i in range(first, length) if 0 <= i + by < length]
    return lax.ppermute(x, axis, pairs)


def after(value, *others):
    return lax.optimization_barrier((value,) + others)[0]


def row_split_refresh(grad_term_sum, moment, left_old, left_new, right_old, right_new):
    turn_share = lax.psum_scatter(
        jnp.einsum("brk,brj->kbj", right_old, right_new, preferred_element_type=jnp.float32),
        "seq", scatter_dimension=0, tiled=True)
    right_turn = jnp.transpose(turn_share, (1, 0, 2)).astype(jnp.bfloat16)
    turned = jnp.einsum(
        "brk,bkj->brj", moment, lax.all_gather(right_turn, "seq", axis=1, tiled=True),
        preferred_element_type=jnp.float32).astype(jnp.bfloat16)
    carried = jnp.einsum(
        "brk,bkj->brj", left_old, lax.all_gather(turned, "seq", axis=1, tiled=True),
        preferred_element_type=jnp.float32)
    grad_term = jnp.einsum(
        "brk,bkj->brj", grad_term_sum, lax.all_gather(right_new, "seq", axis=1, tiled=True),
        preferred_element_type=jnp.float32)
    inner = (moment_decay * carried + (1.0 - moment_decay) * grad_term).astype(jnp.bfloat16)
    new_share = lax.psum_scatter(
        jnp.einsum("brk,brj->kbj", left_new, inner, preferred_element_type=jnp.float32),
        "seq", scatter_dimension=0, tiled=True)
    return jnp.transpose(new_share, (1, 0, 2))


def bmm(spec, a, b):
    return jnp.einsum(spec, a, b, preferred_element_type=jnp.float32)


def pack_body(owner_ref, *refs):
    del owner_ref
    for i, ref in enumerate(refs[:-1]):
        refs[-1][i] = ref[:, 0]


def pack(owner, arrays):
    heads, _, blocks, rows, order = arrays[0].shape
    shape = (len(arrays), heads, blocks, rows, order)
    return pl.pallas_call(
        pack_body,
        out_shape=jax.ShapeDtypeStruct(shape, arrays[0].dtype),
        grid_spec=pltpu.PrefetchScalarGridSpec(
            num_scalar_prefetch=1,
            grid=(1,),
            in_specs=[pl.BlockSpec(
                (heads, 1, blocks, rows, order), lambda i, who: (0, who[0], 0, 0, 0))] * len(arrays),
            out_specs=pl.BlockSpec(shape, lambda i, who: (0,) * 5),
        ),
        compiler_params=pltpu.CompilerParams(vmem_limit_bytes=32 << 20),
        cost_estimate=pl.CostEstimate(
            flops=1 << 20, bytes_accessed=4 << 20, transcendentals=0),
        name="pack_blocks",
    )(jnp.reshape(owner, (1,)).astype(jnp.int32), *arrays)


def project(columns, layer_input):
    return bmm("tj,tk->jk", columns, layer_input).astype(jnp.bfloat16)


def swap_sum(term, n, width):
    index = lax.axis_index("seq")
    if n & (n - 1):
        parts = jnp.stack([term[:, i * width:(i + 1) * width] for i in range(n)])
        return jnp.sum(lax.all_to_all(parts, "seq", 0, 0).astype(jnp.float32), axis=0)
    pieces = [lax.dynamic_slice_in_dim(term, 0, width, 1)] if n == 1 else None
    step = 1
    while step < n:
        mine = (index // step) % 2
        if pieces is None:
            starts = range(n // 2)
            keep = [lax.dynamic_slice_in_dim(term, (2 * i + mine) * width, width, 1) for i in starts]
            send = [lax.dynamic_slice_in_dim(term, (2 * i + 1 - mine) * width, width, 1) for i in starts]
            keep, send = jnp.stack(keep), jnp.stack(send)
        else:
            pairs = pieces.reshape((pieces.shape[0] // 2, 2) + pieces.shape[1:])
            keep = lax.dynamic_index_in_dim(pairs, mine, 1, False)
            send = lax.dynamic_index_in_dim(pairs, 1 - mine, 1, False).astype(jnp.bfloat16)
        got = lax.ppermute(send, "seq", [(i, i ^ step) for i in range(n)])
        pieces = keep.astype(jnp.float32) + got.astype(jnp.float32)
        step *= 2
    return pieces[0].astype(jnp.float32)


def per_device(
    queries, keys, values, out_grad, layer_input, moment, left_old, left_new, right_old, right_new
):
    n = lax.axis_size("seq")
    reach = n // 2
    seq_index = lax.axis_index("seq")
    rows = queries.shape[0]
    hd = HEAD_DIM
    kv_count = keys.shape[1] // hd
    group = queries.shape[1] // keys.shape[1]
    blocks, share_rows, order = moment.shape
    row_blocks = layer_input.shape[1] // order
    whole_blocks = row_blocks % n == 0 and (group + 2) * hd == order
    per_owner = row_blocks // n

    pairs = [
        jnp.concatenate([keys[:, k * hd:(k + 1) * hd], values[:, k * hd:(k + 1) * hd]], axis=1)
        for k in range(kv_count)
    ]
    skip = jnp.reshape(reach - seq_index, (1,)).astype(jnp.int32)

    windows = []
    gate = None
    for k in range(kv_count):
        held = pairs[k] if gate is None else after(pairs[k], gate)
        shards = [pairs[k]]
        if k == 0:
            for hop in range(reach):
                held = shifted(held, "seq", 1, hop)
                shards.insert(0, held)
            gate = held
        else:
            for d in range(1, reach + 1):
                shards.insert(0, shifted(held, "seq", d))
        windows.append(shards)

    if whole_blocks:
        cut = [
            x.reshape(kv_count, n, per_owner, share_rows, order)
            for x in (moment, left_old, left_new, right_old, right_new)
        ]

        def message(owner):
            return jnp.stack([
                lax.dynamic_slice_in_dim(x, owner, 1, 1)[:, 0] for x in cut])

        whole = jnp.zeros((5, kv_count, per_owner, n, share_rows, order), jnp.bfloat16)
        whole = lax.dynamic_update_slice_in_dim(
            whole, message(seq_index)[:, :, :, None], seq_index, 3)
        leftward = []
        for d in range(1, n):
            owner = (seq_index + n - d) % n
            packed = after(message(owner), leftward[0]) if d > 1 else pack(owner, cut)
            leftward.append(shifted(packed, "seq", -d))
        rightward = []
    outs, query_grads, key_grads, value_grads, joined = [], [], [], [], []
    parts_sent = []
    for k in range(kv_count):
        last = k == kv_count - 1
        gate = skip
        if whole_blocks and k < 2:
            gate = after(skip, *(leftward[1:] if k else leftward[:1]))
        head_out, head_dq, *grads = attention(queries, out_grad, gate, windows[k], k, group)
        far, own = grads[:reach], grads[reach]
        outs.append(head_out)
        query_grads.append(head_dq)
        if whole_blocks and k == 0:
            for d in range(1, n):
                packed = after(message((seq_index + d) % n), head_out)
                rightward.append(shifted(packed, "seq", d))
        if not last:
            for d in range(1, reach + 1):
                own = own + shifted(far[reach - d], "seq", -d).astype(jnp.float32)
        else:
            if whole_blocks:
                early = jnp.concatenate(joined + [head_dq], axis=1)
                early_term = swap_sum(project(early, layer_input), n, per_owner * order)
            carry = far[0]
            for d in range(reach, 0, -1):
                carry = shifted(carry, "seq", -1, d)
                if whole_blocks and d == reach:
                    whole = after(whole, carry)
                if d > 1:
                    carry = (carry.astype(jnp.float32) + far[reach - d + 1].astype(jnp.float32)).astype(jnp.bfloat16)
            if whole_blocks:
                for d in range(1, n):
                    source = (seq_index + d) % n
                    piece = jnp.where(seq_index + d < n, leftward[d - 1], rightward[n - d - 1])
                    whole = lax.dynamic_update_slice_in_dim(whole, piece[:, :, :, None], source, 3)
                m_own, lo_own, ln_own, ro_own, rn_own = whole.reshape(
                    5, kv_count, per_owner, order, order)
                right_turn = bmm("cbrk,cbrj->cbkj", ro_own, rn_own).astype(jnp.bfloat16)
                turned = bmm("cbrk,cbkj->cbrj", m_own, right_turn).astype(jnp.bfloat16)
                carried = moment_decay * bmm("cbrk,cbkj->cbrj", lo_own, turned)
                carry = after(carry, carried)
            own = own + carry.astype(jnp.float32)
        kv_grad = own.astype(jnp.bfloat16)
        key_grads.append(kv_grad[:, :hd])
        value_grads.append(kv_grad[:, hd:])
        joined.append(jnp.concatenate([head_dq, kv_grad], axis=1))
    if whole_blocks:
        late_term = swap_sum(project(kv_grad, layer_input), n, per_owner * order)
        grads = jnp.concatenate([early_term, late_term], axis=0).astype(jnp.bfloat16)
        news = []
        for k in range(kv_count):
            grad = grads[k * order:(k + 1) * order].reshape(order, per_owner, order)
            inner = carried[k] + (1.0 - moment_decay) * bmm("jbr,bjk->brk", grad, rn_own[k])
            new = bmm("brk,brj->bkj", ln_own[k], inner.astype(jnp.bfloat16)).astype(jnp.bfloat16)
            new = jnp.transpose(new.reshape(per_owner, n, share_rows, order), (1, 0, 2, 3))
            new = lax.all_to_all(new, "seq", 0, 0)
            news.append(new.reshape(row_blocks, share_rows, order).astype(jnp.float32))
    if whole_blocks:
        new_moment = jnp.concatenate(news, axis=0)
    else:
        joined = jnp.concatenate(joined, axis=1)
        term = bmm(
            "trk,tcj->kcrj",
            layer_input.reshape(rows, row_blocks, order),
            joined.reshape(rows, joined.shape[1] // order, order))
        share = lax.psum_scatter(
            term.reshape(order, blocks, order), "seq", scatter_dimension=0, tiled=True)
        new_moment = row_split_refresh(
            jnp.transpose(share, (1, 0, 2)).astype(jnp.bfloat16),
            moment, left_old, left_new, right_old, right_new)
    join = lambda parts: parts[0] if len(parts) == 1 else jnp.concatenate(parts, axis=1)
    return (join(outs), join(query_grads), join(key_grads), join(value_grads), new_moment)


def solution(mesh):
    both = P(("groups", "seq"), "grid")
    block = P(("groups", "grid"), "seq", None)
    return jax.shard_map(
        per_device,
        mesh=mesh,
        in_specs=(both, both, both, both, P(("groups", "seq"), None)) + (block,) * 5,
        out_specs=(both, both, both, both, block),
        check_vma=False,
    )
```
